128 devices in a mesh: head: 4 (over y), req: 32 (over x, z, core).
Axes of the slice: x: 4, y: 4, z: 4, core: 2. Of those that a mesh axis runs over, the one named last changes fastest.
Arguments:
- hidden_in: bfloat16 [512, 2048], P('req'), may hold values from -40 to 40
- gain_attn: float32 [2048], replicated, may hold values from 0.1 to 1.9
- gain_moe: float32 [2048], replicated, may hold values from 0.1 to 1.9
- w_query: bfloat16 [2048, 2048], P(None, 'head'), may hold values from -0.125 to 0.125
- w_key: bfloat16 [2048, 2048], P(None, 'head'), may hold values from -0.125 to 0.125
- w_value: bfloat16 [2048, 2048], P(None, 'head'), may hold values from -0.125 to 0.125
- w_out: bfloat16 [2048, 2048], P('head'), may hold values from -0.47851562 to 0.47851562
- w_router: bfloat16 [2048, 64], replicated, may hold values from -32 to 32
- w_gate: bfloat16 [64, 2048, 1024], P('req', None, 'head'), may hold values from -0.125 to 0.125
- w_up: bfloat16 [64, 2048, 1024], P('req', None, 'head'), may hold values from -0.125 to 0.125
- w_down: bfloat16 [64, 1024, 2048], P('req', 'head'), may hold values from -1.5 to 1.5
- cache_kv: bfloat16 [2, 256, 256, 2048], P(None, 'req', None, 'head'), may hold values from -210 to 210
- parked_kv: bfloat16 [2, 256, 256, 2048], P(None, 'req', None, 'head'), may hold values from -210 to 210
- lengths: int32 [512], replicated, may hold values from 1 to 256, 65536 in all
- cache_source: int32 [256], replicated, may hold values from 0 to 255, each once
- expert_ids: int32 [512, 8], P('req'), may hold values from 0 to 63, all different within a row; in each aligned block of 16 rows (0 to 15, 16 to 31, ...) at most 4 rows name the same one
Outputs:
- layer_out: bfloat16 [512, 2048], P('req', 'head')
The draws below stay inside these ranges and needn't reach their ends.
Inputs may be any that keep to these rules, and one draw needn't show every extreme that they name: `cache_source`: every parked row belongs to exactly one continuing request. `expert_ids`: in each aligned block of 16 rows no expert is named by more than 4 rows, a bound that some block reaches.
All inputs are finite; a program needn't handle non-finite values.
Results may differ from the reference program's by a relative error of at most 0.025.
Values may be sent and summed in bfloat16 or wider, within the bound.
A program may use at most 128 MiB of HBM per device.

```python
import math
import jax
import jax.numpy as jnp
import numpy as np
from jax import lax

D = 2048
H = 16
FF = 1024
E = 64
TOPK = 8
R_DEV = 16
MAXLEN = 256
HD = 128
RES = 8
CAP = 4
REQS = 512
CONT = 256
N_REQ = 32


def log_spread(key, shape, low, high):
    return jnp.exp(jax.random.uniform(key, shape, jnp.float32, math.log(low), math.log(high)))


def draw_hidden_in(key, part):
    first, second, third = jax.random.split(key, 3)
    base = jnp.clip(jax.random.normal(first, (REQS, D), jnp.float32), -4.0, 4.0)
    row_scale = log_spread(second, (REQS, 1), 0.15, 1.5)
    col_scale = log_spread(third, (1, D), 0.3, 3.0)
    return (base * row_scale * col_scale).astype(jnp.bfloat16)


def draw_w_router(key, part):
    first, second = jax.random.split(key, 2)
    col_scale = log_spread(second, (1, E), 0.4, 1.2)
    base = jnp.clip(jax.random.normal(first, (D, E), jnp.float32), -5.0, 5.0)
    values = base * col_scale * D ** (-0.5)
    return values.astype(jnp.bfloat16)


def cache_like(key):
    first = jax.random.fold_in(key, 0)
    shape = (2, CONT, MAXLEN, D)
    base = jnp.clip(jax.random.normal(first, shape, jnp.float32), -6.0, 6.0) * 2.0
    return base.astype(jnp.bfloat16)


def draw_cache_kv(key, part):
    return cache_like(jax.random.fold_in(key, 11))


def draw_parked_kv(key, part):
    return cache_like(jax.random.fold_in(key, 23))


def levels(rng, extent, shards, low, top_value):
    loudness, own = 1.0, jax.random.fold_in(rng, 6)
    for dim, blocks in shards:
        draws = jnp.exp(jax.random.uniform(jax.random.fold_in(own, dim), (blocks,), jnp.float32, low / len(shards), top_value / len(shards)))
        loudness = loudness * jnp.repeat(draws, extent[dim] // blocks).reshape([-1 if axis == dim else 1 for axis in range(len(extent))])
    return loudness


def split_up(number_of, total, most, skew):
    weights = [(1 << 20) // math.isqrt(standing ** skew) + 1 for standing in range(2, number_of + 1)]
    rest, counts = total - most - (number_of - 1), [1] * (number_of - 1)
    while rest > 0:
        movable = [i for i in range(number_of - 1) if counts[i] < most]
        pool, left = sum([weights[i] for i in movable]), rest
        for i in movable:
            more = min(most - counts[i], max(1, left * weights[i] // pool), rest)
            counts[i] = counts[i] + more
            rest = rest - more
    return np.array([most] + counts)


def uneven(key, number_of, total, most, lean):
    if number_of == 2:
        one = jax.random.randint(key, (), max(1, total - most), min(most, total - 1) + 1)
        return jnp.stack([one, total - one])
    tallies = jnp.asarray(split_up(number_of, total, most, lean), jnp.int32)
    pairs = (number_of - 1) // 2
    source_of, sink = tallies[1:1 + 2 * pairs:2], tallies[2:2 + 2 * pairs:2]
    slack = jnp.minimum(source_of - 1, most - sink)
    passed = jax.random.randint(jax.random.fold_in(key, 1), (pairs,), 0, 1 << 20) % (slack + 1)
    tallies = tallies.at[1:1 + 2 * pairs:2].set(source_of - passed).at[2:2 + 2 * pairs:2].set(sink + passed)
    return tallies[jax.random.permutation(jax.random.fold_in(key, 2), number_of)]


def routed_block(own_key, own, number, rows, number_of, top, limit, lean):
    order = jax.random.permutation(own_key, number_of)
    heavy_load, ordinary = load_shares(number_of, rows * top, limit, lean, True), load_shares(number_of, rows * top, limit, lean, False)
    places = jnp.arange(number_of)

    def named(sizes, offset_by):
        used = int((sizes > 0).sum())
        fixed = max(1, used // 4)
        passed = fixed + (places - fixed + offset_by * (used - fixed)) % max(1, number_of - fixed)
        return jnp.zeros((number_of,), jnp.int32).at[order[jnp.where(places < fixed, places, passed)]].set(jnp.asarray(sizes, jnp.int32))

    sizes = jnp.where(number % 4 == 0, named(heavy_load, number // 4), named(ordinary, number - number // 4 - 1))
    mixed = jax.random.permutation(jax.random.fold_in(own, 3), number_of)
    source_of, receiver = mixed[0:number_of // 2 * 2:2], mixed[1:number_of // 2 * 2:2]
    slack = jnp.minimum(sizes[source_of] - 1, limit - sizes[receiver]) // 2
    slack = jnp.where((source_of == order[0]) | (receiver == order[0]) | (sizes[receiver] == 0), 0, jnp.maximum(slack, 0))
    passed = jax.random.randint(jax.random.fold_in(own, 4), (number_of // 2,), 0, 1 << 20) % (slack + 1)
    sizes = sizes.at[source_of].add(-passed).at[receiver].add(passed)
    items = jnp.searchsorted(jnp.cumsum(sizes), jnp.arange(rows * top), side="right").astype(jnp.int32)
    grid = items.reshape(top, rows).T
    grid = grid[jax.random.permutation(jax.random.fold_in(own, 1), rows)]
    offset_by = jax.random.randint(jax.random.fold_in(own, 2), (rows, 1), 0, top)
    return jnp.take_along_axis(grid, (jnp.arange(top)[None, :] + offset_by) % top, axis=1)


def load_shares(amount, total, bound, skew, full):
    portions = [(1 << 20) // math.isqrt(grade ** skew) + 1 for grade in range(1, amount + 1)]
    largest = bound if full else min(bound, max(-(-total // amount), total * portions[0] // sum(portions)))
    least = 1 if total - largest >= amount - 1 else 0
    given, surplus = [largest] + [least] * (amount - 1), total - largest - least * (amount - 1)
    while surplus > 0:
        candidates = [i for i in range(1, amount) if given[i] < largest] or [i for i in range(1, amount) if given[i] < bound]
        whole, left = sum([portions[i] for i in candidates]), surplus
        for i in candidates:
            more = min(bound - given[i], max(1, left * portions[i] // whole), surplus)
            given[i] = given[i] + more
            surplus = surplus - more
    return np.array(given)


def scatter_about(key, shape, width, limit, cuts=(), kind=jnp.bfloat16):
    loudness = levels(key, shape, cuts, -0.22, 0.18) if cuts else 1.0
    entries = jax.random.normal(key, shape, jnp.float32) * width * loudness
    return jnp.minimum(jnp.maximum(entries, -limit), limit).astype(kind)


def setup_inputs(seed: int = 0) -> dict:
    streams_of = jax.random.split(jax.random.key(seed), 17)
    hidden_in = draw_hidden_in(jax.random.fold_in(streams_of[16], 71), 0)
    gain_attn = jnp.clip(1.0 + 0.18 * jax.random.normal(streams_of[1], (D,), jnp.float32), 0.1, 1.9)
    gain_moe = jnp.clip(1.0 + 0.18 * jax.random.normal(streams_of[2], (D,), jnp.float32), 0.1, 1.9)
    w_query = scatter_about(streams_of[3], (D, D), D ** -0.5, 0.125, ((1, 4),))
    w_key = scatter_about(streams_of[4], (D, D), D ** -0.5, 0.125, ((1, 4),))
    w_value = scatter_about(streams_of[5], (D, D), D ** -0.5, 0.125, ((1, 4),))
    w_out = scatter_about(streams_of[6], (D, D), 0.08, 0.47851562, ((0, 4),))
    w_router = draw_w_router(jax.random.fold_in(streams_of[16], 71), 0)
    w_gate = scatter_about(streams_of[8], (E, D, FF), D ** -0.5, 0.125, ((0, 32), (2, 4)))
    w_up = scatter_about(streams_of[9], (E, D, FF), D ** -0.5, 0.125, ((0, 32), (2, 4)))
    w_down = scatter_about(streams_of[10], (E, FF, D), (FF // 64) ** -0.5, 1.5, ((0, 32), (1, 4)))
    cache_kv = draw_cache_kv(jax.random.fold_in(streams_of[16], 71), 0)
    parked_kv = draw_parked_kv(jax.random.fold_in(streams_of[16], 71), 0)
    lengths = uneven(streams_of[13], REQS, REQS * MAXLEN // 2, MAXLEN, 2).astype(jnp.int32)
    cache_source = jax.random.permutation(streams_of[14], CONT).astype(jnp.int32)
    expert_ids_keys = jax.random.split(jax.random.fold_in(streams_of[15], 1), REQS // R_DEV)
    expert_ids_turns = jax.random.permutation(jax.random.fold_in(streams_of[15], 3), REQS // R_DEV)
    expert_ids = jax.vmap(lambda own, number: routed_block(jax.random.fold_in(streams_of[15], 2), own, number, R_DEV, E, TOPK, CAP, 2))(expert_ids_keys, expert_ids_turns).reshape((REQS, TOPK))
    return {"hidden_in": hidden_in, "gain_attn": gain_attn, "gain_moe": gain_moe, "w_query": w_query, "w_key": w_key, "w_value": w_value, "w_out": w_out, "w_router": w_router, "w_gate": w_gate, "w_up": w_up, "w_down": w_down, "cache_kv": cache_kv, "parked_kv": parked_kv, "lengths": lengths, "cache_source": cache_source, "expert_ids": expert_ids}


epsilon = 1e-06
rope_base = 50000.0

def rms_scale(inputs, gain):
    inputs = inputs.astype(jnp.float32)
    inverse = lax.rsqrt(lax.optimization_barrier(jnp.mean(inputs * inputs, axis=-1, keepdims=True)) + epsilon)
    return inputs * inverse * gain.astype(jnp.float32)

def rotate(vectors, positions):
    half_dim = vectors.shape[-1] // 2
    frequency = rope_base ** (-2.0 * jnp.arange(half_dim, dtype=jnp.float32) / vectors.shape[-1])
    angles = positions.astype(jnp.float32)[:, None] * frequency[None, :]
    cosine = jnp.cos(angles)[:, None, :]
    sine_part = jnp.sin(angles)[:, None, :]
    leading = vectors[..., :half_dim]
    trailing = vectors[..., half_dim:]
    return jnp.concatenate([leading * cosine - trailing * sine_part, trailing * cosine + leading * sine_part], axis=-1)

def cache_part(one_query, key_rows, value_rows, one_length):
    scores = jnp.einsum('hd,jhd->hj', one_query.astype(jnp.float32), key_rows.astype(jnp.float32)) * HD ** (-0.5)
    usable = (jnp.arange(MAXLEN, dtype=jnp.int32) < one_length)[None, :]
    scores = jnp.where(usable, scores, -1e+30)
    row_max = lax.optimization_barrier(jnp.max(scores, axis=-1))
    weights = jnp.where(usable, jnp.exp(scores - row_max[:, None]), 0.0)
    row_total = lax.optimization_barrier(jnp.sum(weights, axis=-1))
    probs = weights.astype(jnp.bfloat16).astype(jnp.float32)
    weighted = jnp.einsum('hj,jhd->hd', probs, value_rows.astype(jnp.float32))
    return (weighted, row_max, row_total)

def finish(weighted, row_max, row_total, queries, key_new, value_new):
    new_score = lax.optimization_barrier(jnp.sum(queries.astype(jnp.float32) * key_new.astype(jnp.float32), axis=-1)) * queries.shape[-1] ** (-0.5)
    joint_max = jnp.maximum(row_max, new_score)
    old_part = jnp.exp(row_max - joint_max)
    new_part = jnp.exp(new_score - joint_max)
    numerator = weighted * old_part[..., None] + new_part[..., None] * value_new.astype(jnp.float32)
    return numerator / (row_total * old_part + new_part)[..., None]

def attend(source_cache):

    def single(packed):
        one_query, row_index, one_length = packed
        cache_rows = lax.dynamic_index_in_dim(source_cache, row_index, axis=1, keepdims=False)
        key_rows = cache_rows[0].reshape(MAXLEN, H, HD)
        value_rows = cache_rows[1].reshape(MAXLEN, H, HD)
        return cache_part(one_query, key_rows, value_rows, one_length)
    return single

def regroup(home_part, away_part):
    tail_shape = home_part.shape[1:]
    joined = jnp.concatenate([home_part.reshape((N_REQ, RES) + tail_shape), away_part.reshape((N_REQ, RES) + tail_shape)], axis=1)
    return joined.reshape((REQS,) + tail_shape)

def reference(hidden_in, gain_attn, gain_moe, w_query, w_key, w_value, w_out, w_router, w_gate, w_up, w_down, cache_kv, parked_kv, lengths, cache_source, expert_ids):
    normed_attn = rms_scale(hidden_in, gain_attn).astype(jnp.bfloat16)
    queries = jnp.dot(normed_attn, w_query, preferred_element_type=jnp.float32).reshape(REQS, H, HD)
    queries = rotate(queries, lengths).astype(jnp.bfloat16)
    key_new = jnp.dot(normed_attn, w_key, preferred_element_type=jnp.float32).reshape(REQS, H, HD)
    key_new = rotate(key_new, lengths).astype(jnp.bfloat16)
    value_new = jnp.dot(normed_attn, w_value, preferred_element_type=jnp.float32).astype(jnp.bfloat16).reshape(REQS, H, HD)
    grid_queries = queries.reshape(N_REQ, R_DEV, H, HD)
    home_queries = grid_queries[:, :RES].reshape(CONT, H, HD)
    moving_queries = grid_queries[:, RES:].reshape(CONT, H, HD)
    grid_lengths = lengths.reshape(N_REQ, R_DEV)
    home_lengths = grid_lengths[:, :RES].reshape(CONT)
    moving_lengths = grid_lengths[:, RES:].reshape(CONT)
    home = lax.map(attend(cache_kv), (home_queries, jnp.arange(CONT, dtype=jnp.int32), home_lengths))
    away = lax.map(attend(parked_kv), (moving_queries, cache_source.astype(jnp.int32), moving_lengths))
    weighted = regroup(home[0], away[0])
    row_max = regroup(home[1], away[1])
    row_total = regroup(home[2], away[2])
    attended = finish(weighted, row_max, row_total, queries, key_new, value_new).astype(jnp.bfloat16).reshape(REQS, D)
    residual = hidden_in.astype(jnp.float32) + jnp.dot(attended, w_out, preferred_element_type=jnp.float32)
    normed_moe = rms_scale(residual, gain_moe).astype(jnp.bfloat16)
    logits = jnp.dot(normed_moe, w_router, preferred_element_type=jnp.float32)
    gate_values = jax.nn.softmax(jnp.take_along_axis(logits, expert_ids, axis=1), axis=-1)
    slot_total = N_REQ * CAP

    def one_expert(running, packed):
        gate_w, up_w, down_w, expert = packed
        chosen_mask = expert_ids == expert
        token_gate = lax.optimization_barrier(jnp.sum(jnp.where(chosen_mask, gate_values, 0.0), axis=1))
        routed = jnp.any(chosen_mask, axis=1)
        row_index = jnp.nonzero(routed, size=slot_total, fill_value=0)[0].astype(jnp.int32)
        routed_count = jnp.sum(routed.astype(jnp.int32))
        in_use = jnp.arange(slot_total, dtype=jnp.int32) < routed_count
        picked = normed_moe[row_index]
        gate_part = jnp.dot(picked, gate_w, preferred_element_type=jnp.float32)
        up_part = jnp.dot(picked, up_w, preferred_element_type=jnp.float32)
        hidden = (jax.nn.silu(gate_part) * up_part).astype(jnp.bfloat16)
        expert_out = jnp.dot(hidden, down_w, preferred_element_type=jnp.float32)
        scale_rows = jnp.where(in_use, token_gate[row_index], 0.0)
        return (running.at[row_index].add(expert_out * scale_rows[:, None]), None)
    mixture, unused = lax.scan(one_expert, jnp.zeros((REQS, D), jnp.float32), (w_gate, w_up, w_down, jnp.arange(E, dtype=jnp.int32)))
    return (residual + mixture).astype(jnp.bfloat16)
```

```python
import jax
import jax.numpy as jnp
import numpy as np
from jax import lax
from jax.experimental import pallas as pl
from jax.experimental.pallas import tpu as pltpu
from jax.sharding import PartitionSpec as P

MESH = pl.DeviceIdType.MESH
F32 = jnp.float32
BF16 = jnp.bfloat16
I32 = jnp.int32

D = 2048
HD = 128
E = 64
NREQ = 32
NHEAD = 4
ROWS = 16
RES = 8
SPAN = 256
WIDTH = 512
FFL = 256
SCALE = HD ** (-0.5)
EPS = 1e-06


def iota(shape, dim):
    return lax.broadcasted_iota(I32, shape, dim)


def rms_scale(x, gain):
    inverse = lax.rsqrt(jnp.mean(x * x, axis=-1, keepdims=True) + EPS)
    return x * inverse * gain


def round_trip(x):
    return x.astype(BF16).astype(F32)


def dot(a, b):
    return jnp.dot(a, b, preferred_element_type=F32)


def rotate(x, cosine, sine):
    parts = []
    for h in range(NHEAD):
        u = x[:, h * HD:(h + 1) * HD]
        parts.append(u * cosine + pltpu.roll(u, HD // 2, 1) * sine)
    return jnp.concatenate(parts, axis=1)


def cache_attention(q, row_lengths, kv):
    stacked = jnp.concatenate([q] * NHEAD, axis=0)
    row = iota((NHEAD * RES, WIDTH), 0)
    col = iota((NHEAD * RES, WIDTH), 1)
    stacked = jnp.where(row // RES == col // HD, stacked, 0.0)
    scores = jnp.zeros((NHEAD * RES, SPAN), F32)
    for i in range(RES):
        part = jnp.where(row % RES == i, stacked, 0.0).astype(BF16)
        scores = scores + lax.dot_general(
            part, kv[0, i], (((1,), (1,)), ((), ())), preferred_element_type=F32)
    scores = scores * SCALE
    limit = jnp.concatenate([row_lengths] * NHEAD, axis=0)
    usable = iota((NHEAD * RES, SPAN), 1).astype(F32) < limit
    scores = jnp.where(usable, scores, -1e30)
    row_max = jnp.max(scores, axis=1, keepdims=True)
    weights = jnp.where(usable, jnp.exp(scores - row_max), 0.0)
    row_total = jnp.sum(weights, axis=1, keepdims=True)
    probs = weights.astype(BF16)
    pieces = [jnp.zeros((RES, HD), F32)] * NHEAD
    small = iota((RES, HD), 0)
    for i in range(RES):
        out = dot(probs, kv[1, i])
        for h in range(NHEAD):
            pieces[h] = jnp.where(
                small == i, out[h * RES:(h + 1) * RES, h * HD:(h + 1) * HD], pieces[h])
    maxes = [row_max[h * RES:(h + 1) * RES] for h in range(NHEAD)]
    totals = [row_total[h * RES:(h + 1) * RES] for h in range(NHEAD)]
    normal = [pieces[h] / totals[h] for h in range(NHEAD)]
    return normal, maxes, totals


def kernel(
    hidden_ref, gain_a_ref, gain_m_ref, freq_ref, lengths_ref, source_ref, ids_ref,
    wq_hbm, wk_hbm, wv_hbm, wo_hbm, wr_hbm, wg_hbm, wu_hbm, wd_hbm, cache_hbm, parked_hbm,
    out_ref,
    wq, wk, wv, wo, wr, wg, wu, wd, cache, parked,
    q_send, q_all, a_send, a_all, head_all, disp, arrived, ret_send, ret, fin_send, fin_all, resid,
    load_sem, q_ss, q_rs, a_ss, a_rs, h_ss, h_rs, d_ss, d_rs, r_ss, r_rs, f_ss, f_rs,
):
    me = lax.axis_index("req")
    head = lax.axis_index("head")

    loads = {}
    order = [("wq", wq_hbm, wq), ("wk", wk_hbm, wk), ("wv", wv_hbm, wv), ("cache", cache_hbm, cache),
             ("parked", parked_hbm, parked), ("wo", wo_hbm, wo), ("wr", wr_hbm, wr),
             ("wg", wg_hbm, wg), ("wu", wu_hbm, wu), ("wd", wd_hbm, wd)]
    for n, (name, src, dst) in enumerate(order):
        loads[name] = pltpu.make_async_copy(src, dst, load_sem.at[n])
        loads[name].start()

    barrier = pltpu.get_barrier_semaphore()

    def hello(d, carry):
        pl.semaphore_signal(barrier, inc=1, device_id={"req": (me + d) % NREQ}, device_id_type=MESH)
        return carry

    lax.fori_loop(1, NREQ, hello, 0)
    for d in range(1, NHEAD):
        pl.semaphore_signal(barrier, inc=1, device_id={"head": (head + d) % NHEAD}, device_id_type=MESH)

    def exchange(axis, count, mine, block_of, landing, ss, rs):
        def copy(d):
            peer = (mine + d) % count
            return pltpu.make_async_remote_copy(
                src_ref=block_of(peer), dst_ref=landing.at[mine], send_sem=ss.at[d], recv_sem=rs.at[mine],
                device_id={axis: peer}, device_id_type=MESH)

        def start(d, carry):
            copy(d).start()
            return carry

        lax.fori_loop(1, count, start, 0)

        def finish_recv(d, carry):
            other = (mine + d) % count
            pltpu.make_async_remote_copy(
                src_ref=block_of(other), dst_ref=landing.at[other], send_sem=ss.at[d], recv_sem=rs.at[other],
                device_id={axis: other}, device_id_type=MESH).wait_recv()
            return carry

        def finish_send(d, carry):
            copy(d).wait_send()
            return carry

        return (lambda: lax.fori_loop(1, count, finish_recv, 0),
                lambda: lax.fori_loop(1, count, finish_send, 0))

    hidden = hidden_ref[...].astype(F32)
    normed = rms_scale(hidden, gain_a_ref[...]).astype(BF16)
    pick = iota((ROWS, NREQ * ROWS), 1) == me * ROWS + iota((ROWS, NREQ * ROWS), 0)
    own_len = jnp.sum(jnp.where(pick, lengths_ref[...].astype(F32), 0.0), axis=1, keepdims=True)
    angles = own_len * freq_ref[...]
    cosine = jnp.cos(angles)
    sine = jnp.sin(angles)
    sine = jnp.where(iota((ROWS, HD), 1) < HD // 2, -sine, sine)
    loads["wq"].wait()
    q = round_trip(rotate(dot(normed, wq[...]), cosine, sine))

    len_block = jnp.broadcast_to(own_len[RES:], (RES, HD))
    q_block = jnp.concatenate([
        jnp.concatenate([q[RES:, :256], len_block], axis=1),
        jnp.concatenate([q[RES:, 256:], len_block], axis=1)], axis=0).astype(BF16)
    q_send[...] = q_block
    q_all[me] = q_block
    pl.semaphore_wait(barrier, NREQ - 1 + NHEAD - 1)
    q_recv, q_sent = exchange("req", NREQ, me, lambda p: q_send, q_all, q_ss, q_rs)

    loads["wk"].wait()
    k = round_trip(rotate(dot(normed, wk[...]), cosine, sine))
    loads["wv"].wait()
    v = round_trip(dot(normed, wv[...]))

    wide = NREQ * ROWS
    g_row = iota((ROWS, wide), 0)
    g_col = iota((ROWS, wide), 1)
    same_half = g_row // RES == (g_col % ROWS) // RES
    spread = iota((256, wide), 0) == (iota((256, wide), 1) // ROWS) * RES + iota((256, wide), 1) % RES
    source = jnp.broadcast_to(source_ref[...].astype(F32), (RES, 256))
    source_wide = dot(source.astype(BF16), spread.astype(F32).astype(BF16))[0:1]
    hot_park = (same_half & (source_wide == (me * RES + g_row % RES).astype(F32))).astype(F32).astype(BF16)
    pick = iota((ROWS, 256), 1) == me * RES + iota((ROWS, 256), 0) % RES
    own_source = jnp.sum(jnp.where(pick, source_ref[...].astype(F32), 0.0), axis=1, keepdims=True)
    slot = ((g_col // ROWS) * RES + g_col % RES).astype(F32)
    hot_home = (same_half & (own_source == slot)).astype(F32).astype(BF16)

    loads["cache"].wait()
    home_a, home_m, home_t = cache_attention(q[:RES], own_len[:RES], cache)

    q_recv()
    parked_q = dot(hot_park, q_all[...].reshape(wide, 384))
    loads["parked"].wait()
    park_a, park_m, park_t = cache_attention(
        jnp.concatenate([parked_q[:RES, :256], parked_q[RES:, :256]], axis=1), parked_q[:RES, 256:257], parked)

    lane = iota((RES, HD), 1)
    halves = []
    for half in range(2):
        stats = jnp.zeros((RES, HD), F32)
        for w in range(2):
            m, t = park_m[2 * half + w], park_t[2 * half + w]
            m0 = round_trip(m)
            m1 = round_trip(m - m0)
            m2 = m - m0 - m1
            t0 = round_trip(t)
            t1 = t - t0
            for n, value in enumerate((m0, m1, m2, t0, t1)):
                stats = jnp.where(lane == 8 * w + n, value, stats)
        halves.append(jnp.concatenate([park_a[2 * half], park_a[2 * half + 1], stats], axis=1))
    a_block = jnp.concatenate(halves, axis=0).astype(BF16)
    a_send[...] = a_block
    a_all[me] = a_block
    a_recv, a_sent = exchange("req", NREQ, me, lambda p: a_send, a_all, a_ss, a_rs)
    q_sent()

    new_score = [SCALE * jnp.sum(q[:, h * HD:(h + 1) * HD] * k[:, h * HD:(h + 1) * HD], axis=1, keepdims=True)
                 for h in range(NHEAD)]

    ids = ids_ref[...]
    expert = iota((ROWS, E), 1)
    chosen = jnp.zeros((ROWS, E), F32)
    for n in range(ids.shape[1]):
        chosen = jnp.where(ids[:, n:n + 1] == expert, 1.0, chosen)
    lower = (iota((ROWS, ROWS), 1) < iota((ROWS, ROWS), 0)).astype(F32).astype(BF16)
    rank = dot(lower, chosen.astype(BF16))
    e_of = iota((E, wide), 0)
    w_of = iota((E, wide), 1)
    expand = (e_of == (w_of // ROWS) * 2 + (w_of % RES) // 4).astype(F32).astype(BF16)
    placed = dot(jnp.concatenate([chosen, rank], axis=0).astype(BF16), expand)
    taken = jnp.where((placed[:ROWS] > 0.5) & (placed[ROWS:] == (g_col % 4).astype(F32)), 1.0, 0.0)
    low_half = (g_col % ROWS) // RES == 0
    taken_halves = jnp.concatenate([jnp.where(low_half, taken, 0.0), jnp.where(low_half, 0.0, taken)], axis=0)
    taken_t = taken_halves.T.astype(BF16)

    a_recv()
    back = dot(hot_home, a_all[...].reshape(wide, 384))
    pieces = []
    for h in range(NHEAD):
        half, w = h // 2, h % 2
        rows = back[half * RES:(half + 1) * RES]
        st = rows[:, 256 + 8 * w:256 + 8 * w + 5]
        back_m = st[:, 0:1] + st[:, 1:2] + st[:, 2:3]
        back_t = st[:, 3:4] + st[:, 4:5]
        a = jnp.concatenate([home_a[h], rows[:, w * HD:(w + 1) * HD]], axis=0)
        m = jnp.concatenate([home_m[h], back_m], axis=0)
        t = jnp.concatenate([home_t[h], back_t], axis=0)
        top = jnp.maximum(m, new_score[h])
        old = t * jnp.exp(m - top)
        new = jnp.exp(new_score[h] - top)
        total = old + new
        pieces.append(a * (old / total) + v[:, h * HD:(h + 1) * HD] * (new / total))
    attended = jnp.concatenate(pieces, axis=1).astype(BF16)

    loads["wo"].wait()
    terms = dot(attended, wo[...]).astype(BF16)
    head_all[head] = terms
    h_recv, h_sent = exchange("head", NHEAD, head, lambda p: head_all.at[head], head_all, h_ss, h_rs)
    a_sent()
    h_recv()
    residual = hidden + ((head_all[0].astype(F32) + head_all[1].astype(F32))
                         + (head_all[2].astype(F32) + head_all[3].astype(F32)))
    resid[...] = residual
    normed_f = round_trip(rms_scale(residual, gain_m_ref[...]))

    stacked = jnp.concatenate([normed_f[:, :1024], normed_f[:, 1024:]], axis=0).astype(BF16)
    disp[...] = dot(taken_t, stacked).astype(BF16).reshape(NREQ, ROWS, 1024)
    arrived[me] = disp[me]
    d_recv, d_sent = exchange("req", NREQ, me, lambda p: disp.at[p], arrived, d_ss, d_rs)
    h_sent()

    loads["wr"].wait()
    logits = dot(normed_f.astype(BF16), wr[...])
    hit = chosen > 0.5
    top = jnp.max(jnp.where(hit, logits, -3e38), axis=1, keepdims=True)
    power = jnp.where(hit, jnp.exp(jnp.where(hit, logits, top) - top), 0.0)
    gates = power / jnp.sum(power, axis=1, keepdims=True)
    g_hi = round_trip(gates)
    gate_wide = dot(jnp.concatenate([g_hi, gates - g_hi], axis=0).astype(BF16), expand)
    mix_hi = gate_wide[:ROWS] * taken
    mix_lo = gate_wide[ROWS:] * taken
    mix = jnp.concatenate([
        jnp.where(low_half, mix_hi, 0.0), jnp.where(low_half, mix_lo, 0.0),
        jnp.where(low_half, 0.0, mix_hi), jnp.where(low_half, 0.0, mix_lo)], axis=0).astype(BF16)

    loads["wg"].wait()
    loads["wu"].wait()
    loads["wd"].wait()
    d_recv()
    tokens = arrived[...].astype(F32).reshape(NREQ, 2, RES, 1024)
    left = tokens[:, 0].reshape(NREQ * RES, 1024).astype(BF16)
    right = tokens[:, 1].reshape(NREQ * RES, 1024).astype(BF16)
    which = (iota((NREQ * RES, FFL), 0) % RES) // 4
    inner = []
    for e in range(2):
        gate = dot(left, wg[e, :1024]) + dot(right, wg[e, 1024:])
        up = dot(left, wu[e, :1024]) + dot(right, wu[e, 1024:])
        act = gate / (1.0 + jnp.exp(-gate)) * up
        inner.append(jnp.where(which == e, act, 0.0).astype(BF16))
    parts = []
    for half in range(2):
        cols = slice(half * 1024, (half + 1) * 1024)
        y = dot(inner[0], wd[0, :, cols]) + dot(inner[1], wd[1, :, cols])
        parts.append(y.reshape(NREQ, RES, 1024))
    ret_send[...] = jnp.concatenate(parts, axis=1).astype(BF16)
    ret[me] = ret_send[me]
    r_recv, r_sent = exchange("req", NREQ, me, lambda p: ret_send.at[p], ret, r_ss, r_rs)
    d_sent()
    r_recv()
    mixed = dot(mix, ret[...].reshape(wide, 1024))
    mixture = [mixed[0:16] + mixed[16:32], mixed[32:48] + mixed[48:64]]
    for h in range(NHEAD):
        fin_send[h] = mixture[h // 2][:, (h % 2) * WIDTH:(h % 2 + 1) * WIDTH].astype(BF16)
    fin_all[head] = fin_send[head]
    f_recv, f_sent = exchange("head", NHEAD, head, lambda p: fin_send.at[p], fin_all, f_ss, f_rs)
    r_sent()
    f_recv()
    own = resid[:, pl.ds(pl.multiple_of(head * WIDTH, WIDTH), WIDTH)]
    total = own + ((fin_all[0].astype(F32) + fin_all[1].astype(F32))
                   + (fin_all[2].astype(F32) + fin_all[3].astype(F32)))
    out_ref[...] = total.astype(BF16)
    f_sent()


def body(hidden_in, gain_attn, gain_moe, w_query, w_key, w_value, w_out, w_router, w_gate, w_up, w_down,
         cache_kv, parked_kv, lengths, cache_source, expert_ids):
    half = HD // 2
    freq = 50000.0 ** (-2.0 * np.arange(half, dtype=np.float64) / HD)
    freq = jnp.asarray(np.concatenate([freq, freq])[None, :], F32)
    vmem = pl.BlockSpec(memory_space=pltpu.VMEM)
    hbm = pl.BlockSpec(memory_space=pl.ANY)
    dma = pltpu.SemaphoreType.DMA
    big = [w_query, w_key, w_value, w_out, w_router, w_gate, w_up, w_down, cache_kv, parked_kv]
    block = (NREQ, ROWS, 384)
    wide = (NREQ, ROWS, 1024)
    return pl.pallas_call(
        kernel,
        out_shape=jax.ShapeDtypeStruct((ROWS, WIDTH), BF16),
        in_specs=[vmem] * 7 + [hbm] * 10,
        out_specs=vmem,
        scratch_shapes=[pltpu.VMEM(x.shape, x.dtype) for x in big] + [
            pltpu.VMEM(block[1:], BF16), pltpu.VMEM(block, BF16),
            pltpu.VMEM(block[1:], BF16), pltpu.VMEM(block, BF16),
            pltpu.VMEM((NHEAD, ROWS, D), BF16),
            pltpu.VMEM(wide, BF16), pltpu.VMEM(wide, BF16),
            pltpu.VMEM(wide, BF16), pltpu.VMEM(wide, BF16),
            pltpu.VMEM((NHEAD, ROWS, WIDTH), BF16), pltpu.VMEM((NHEAD, ROWS, WIDTH), BF16),
            pltpu.VMEM((ROWS, D), F32),
            dma((10,)),
            dma((NREQ,)), dma((NREQ,)), dma((NREQ,)), dma((NREQ,)),
            dma((NHEAD,)), dma((NHEAD,)),
            dma((NREQ,)), dma((NREQ,)), dma((NREQ,)), dma((NREQ,)),
            dma((NHEAD,)), dma((NHEAD,)),
        ],
        compiler_params=pltpu.CompilerParams(
            collective_id=0, has_side_effects=True, vmem_limit_bytes=60 * 1024 * 1024),
    )(hidden_in, gain_attn.reshape(1, D), gain_moe.reshape(1, D), freq, lengths.reshape(1, -1),
      cache_source.reshape(1, -1), expert_ids,
      w_query, w_key, w_value, w_out, w_router, w_gate, w_up, w_down, cache_kv, parked_kv)


def solution(mesh):
    placed = (
        P("req", None),
        P(),
        P(),
        P(None, "head"),
        P(None, "head"),
        P(None, "head"),
        P("head", None),
        P(),
        P("req", None, "head"),
        P("req", None, "head"),
        P("req", "head", None),
        P(None, "req", None, "head"),
        P(None, "req", None, "head"),
        P(),
        P(),
        P("req", None),
    )
    return jax.shard_map(
        body, mesh=mesh, in_specs=placed, out_specs=P("req", "head"), check_vma=False
    )
```

```python
import jax
import jax.numpy as jnp
import numpy as np
from jax import lax
from jax.experimental import pallas as pl
from jax.experimental.pallas import tpu as pltpu
from jax.sharding import PartitionSpec as P

MESH = pl.DeviceIdType.MESH
F32 = jnp.float32
BF16 = jnp.bfloat16
I32 = jnp.int32

D = 2048
HD = 128
E = 64
NREQ = 32
NHEAD = 4
ROWS = 16
RES = 8
SPAN = 256
WIDTH = 512
FFL = 256
SCALE = HD ** (-0.5)


def ring(step):
    return min(step, 4 - step)


OFFSETS = sorted(
    ((dx, dz, dc) for dx in range(4) for dz in range(4) for dc in range(2)),
    key=lambda o: (-(ring(o[0]) + ring(o[1])), -o[2], abs(o[0] - o[1]), o))
GROUPS = ((0, 10), (10, 22), (22, 32))
EPS = 1e-06


def iota(shape, dim):
    return lax.broadcasted_iota(I32, shape, dim)


def rms_scale(x, gain):
    inverse = lax.rsqrt(jnp.mean(x * x, axis=-1, keepdims=True) + EPS)
    return x * inverse * gain


def round_trip(x):
    return x.astype(BF16).astype(F32)


def dot(a, b):
    return jnp.dot(a, b, preferred_element_type=F32)


def rotate(x, cosine, sine):
    parts = []
    for h in range(NHEAD):
        u = x[:, h * HD:(h + 1) * HD]
        parts.append(u * cosine + pltpu.roll(u, HD // 2, 1) * sine)
    return jnp.concatenate(parts, axis=1)


def cache_attention(q, row_lengths, kv):
    stacked = jnp.concatenate([q] * NHEAD, axis=0)
    row = iota((NHEAD * RES, WIDTH), 0)
    col = iota((NHEAD * RES, WIDTH), 1)
    stacked = jnp.where(row // RES == col // HD, stacked, 0.0)
    scores = jnp.zeros((NHEAD * RES, SPAN), F32)
    for i in range(RES):
        part = jnp.where(row % RES == i, stacked, 0.0).astype(BF16)
        scores = scores + lax.dot_general(
            part, kv[0, i], (((1,), (1,)), ((), ())), preferred_element_type=F32)
    scores = scores * SCALE
    limit = jnp.concatenate([row_lengths] * NHEAD, axis=0)
    usable = iota((NHEAD * RES, SPAN), 1).astype(F32) < limit
    scores = jnp.where(usable, scores, -1e30)
    row_max = jnp.max(scores, axis=1, keepdims=True)
    weights = jnp.where(usable, jnp.exp(scores - row_max), 0.0)
    row_total = jnp.sum(weights, axis=1, keepdims=True)
    probs = weights.astype(BF16)
    pieces = [jnp.zeros((RES, HD), F32)] * NHEAD
    small = iota((RES, HD), 0)
    for i in range(RES):
        out = dot(probs, kv[1, i])
        for h in range(NHEAD):
            pieces[h] = jnp.where(
                small == i, out[h * RES:(h + 1) * RES, h * HD:(h + 1) * HD], pieces[h])
    maxes = [row_max[h * RES:(h + 1) * RES] for h in range(NHEAD)]
    totals = [row_total[h * RES:(h + 1) * RES] for h in range(NHEAD)]
    normal = [pieces[h] / totals[h] for h in range(NHEAD)]
    return normal, maxes, totals


def kernel(
    hidden_hbm, gain_a_hbm, gain_m_hbm, table_hbm, lengths_hbm, source_hbm, ids_hbm,
    wq_hbm, wk_hbm, wv_hbm, wo_hbm, wr_hbm, wg_hbm, wu_hbm, wd_hbm, cache_hbm, parked_hbm,
    out_ref,
    hidden_ref, gain_a_ref, gain_m_ref, table_ref, lengths_ref, source_ref, ids_ref,
    wq, wk, wv, wo, wr, wg, wu, wd, cache, parked,
    q_send, q_all, a_send, a_all, head_all, disp, arrived, ret_send, ret, fin_send, fin_all, resid,
    load_sem, q_ss, q_rs, a_ss, a_rs, h_ss, h_rs, d_ss, d_rs, r_ss, r_rs, f_ss, f_rs,
):
    me = lax.axis_index("req")
    head = lax.axis_index("head")
    my_x, my_z, my_c = me // 8, (me // 2) % 4, me % 2

    def ahead(n):
        dx, dz, dc = OFFSETS[n]
        return ((my_x + dx) % 4) * 8 + ((my_z + dz) % 4) * 2 + (my_c + dc) % 2

    def behind(n):
        dx, dz, dc = OFFSETS[n]
        return ((my_x + 4 - dx) % 4) * 8 + ((my_z + 4 - dz) % 4) * 2 + (my_c + dc) % 2

    barrier = pltpu.get_barrier_semaphore()
    for n in range(NREQ - 1):
        pl.semaphore_signal(barrier, inc=1, device_id={"req": ahead(n)}, device_id_type=MESH)
    for d in range(1, NHEAD):
        pl.semaphore_signal(barrier, inc=1, device_id={"head": (head + d) % NHEAD}, device_id_type=MESH)

    loads = {}
    order = [("hidden", hidden_hbm, hidden_ref), ("gain_a", gain_a_hbm, gain_a_ref),
             ("table", table_hbm, table_ref), ("lengths", lengths_hbm, lengths_ref),
             ("wq", wq_hbm, wq), ("source", source_hbm, source_ref), ("ids", ids_hbm, ids_ref),
             ("gain_m", gain_m_hbm, gain_m_ref),
             ("wk", wk_hbm, wk), ("wv", wv_hbm, wv), ("cache", cache_hbm, cache),
             ("parked", parked_hbm, parked), ("wo", wo_hbm, wo), ("wr", wr_hbm, wr),
             ("wg", wg_hbm, wg), ("wu", wu_hbm, wu), ("wd", wd_hbm, wd)]
    for n, (name, src, dst) in enumerate(order):
        loads[name] = pltpu.make_async_copy(src, dst, load_sem.at[n])
        loads[name].start()

    def launch(lo, hi, source, landing, ss, rs, target):
        hi = min(hi, NREQ - 1)
        for n in range(lo, hi):
            pltpu.make_async_remote_copy(
                src_ref=source(n), dst_ref=landing.at[n], send_sem=ss, recv_sem=rs,
                device_id={"req": target(n)}, device_id_type=MESH).start()
        whole = pltpu.make_async_remote_copy(
            src_ref=landing.at[pl.ds(lo, hi - lo)], dst_ref=landing.at[pl.ds(lo, hi - lo)],
            send_sem=ss, recv_sem=rs, device_id={"req": target(lo)}, device_id_type=MESH)
        return whole.wait_recv, whole.wait_send

    def head_exchange(source, landing, ss, rs):
        def copy(d, own):
            peer = (head + d) % NHEAD
            return pltpu.make_async_remote_copy(
                src_ref=source(peer), dst_ref=landing.at[head if own else peer], send_sem=ss.at[d],
                recv_sem=rs.at[head if own else peer], device_id={"head": peer}, device_id_type=MESH)

        for d in range(1, NHEAD):
            copy(d, True).start()

        def received():
            for d in range(1, NHEAD):
                copy(d, False).wait_recv()

        def sent():
            for d in range(1, NHEAD):
                copy(d, True).wait_send()

        return received, sent

    for name in ("hidden", "gain_a", "table", "lengths"):
        loads[name].wait()
    hidden = hidden_ref[...].astype(F32)
    normed = rms_scale(hidden, gain_a_ref[...]).astype(BF16)
    pick = iota((ROWS, NREQ * ROWS), 1) == me * ROWS + iota((ROWS, NREQ * ROWS), 0)
    lengths = lengths_ref[...].astype(F32)
    own_len = jnp.sum(jnp.where(pick, lengths, 0.0), axis=1, keepdims=True)
    angles = own_len * table_ref[0:1, :HD]
    cosine = jnp.cos(angles)
    sine = jnp.sin(angles)
    sine = jnp.where(iota((ROWS, HD), 1) < HD // 2, -sine, sine)
    loads["wq"].wait()
    q = round_trip(rotate(dot(normed, wq[...]), cosine, sine))
    q_block = jnp.concatenate([q[RES:, :256], q[RES:, 256:]], axis=0).astype(BF16)
    q_send[...] = q_block
    q_all[NREQ - 1] = q_block

    wide = NREQ * ROWS
    g_row = iota((ROWS, wide), 0)
    g_col = iota((ROWS, wide), 1)
    same_half = g_row // RES == (g_col % ROWS) // RES
    step_x = table_ref[1:2, :].astype(I32)
    step_z = table_ref[2:3, :].astype(I32)
    step_c = table_ref[3:4, :].astype(I32)
    src = ((my_x + 4 - step_x) % 4) * 8 + ((my_z + 4 - step_z) % 4) * 2 + (my_c + step_c) % 2
    dst = ((my_x + step_x) % 4) * 8 + ((my_z + step_z) % 4) * 2 + (my_c + step_c) % 2
    place = src * RES + iota((1, wide), 1) % RES
    natural = iota((256, wide), 1)
    spread = jnp.concatenate([
        (iota((256, wide), 0) == place).astype(F32),
        ((iota((256, wide), 0) == (natural // ROWS) * RES + natural % RES)
         & (natural % ROWS >= RES)).astype(F32)], axis=1).astype(BF16)
    loads["source"].wait()
    source = source_ref[...].astype(F32)
    source_wide = dot(jnp.broadcast_to(source, (RES, 256)).astype(BF16), spread)[0:1]
    hot_park = (same_half & (source_wide[:, :wide] == (me * RES + g_row % RES).astype(F32))).astype(F32).astype(BF16)
    row8 = iota((RES, wide), 0)
    hot_len = (source_wide[:, wide:] == (me * RES + row8).astype(F32)) & (iota((RES, wide), 1) % ROWS >= RES)
    park_len = jnp.sum(jnp.where(hot_len, lengths, 0.0), axis=1, keepdims=True)
    pick = iota((ROWS, 256), 1) == me * RES + iota((ROWS, 256), 0) % RES
    own_source = jnp.sum(jnp.where(pick, source, 0.0), axis=1, keepdims=True)
    hot_home = (same_half & (own_source == place.astype(F32))).astype(F32).astype(BF16)

    pl.semaphore_wait(barrier, NREQ - 1 + NHEAD - 1)
    q_recv, q_sent = launch(0, NREQ, lambda n: q_send, q_all, q_ss.at[0], q_rs.at[0], ahead)

    loads["wk"].wait()
    k = round_trip(rotate(dot(normed, wk[...]), cosine, sine))
    loads["wv"].wait()
    v = round_trip(dot(normed, wv[...]))
    loads["cache"].wait()
    home_a, home_m, home_t = cache_attention(q[:RES], own_len[:RES], cache)
    loads["parked"].wait()

    q_recv()
    parked_q = dot(hot_park, q_all[...].reshape(wide, 256))
    park_a, park_m, park_t = cache_attention(
        jnp.concatenate([parked_q[:RES], parked_q[RES:]], axis=1), park_len, parked)

    lane = iota((RES, HD), 1)
    halves = []
    for half in range(2):
        stats = jnp.zeros((RES, HD), F32)
        for w in range(2):
            m, t = park_m[2 * half + w], park_t[2 * half + w]
            m0 = round_trip(m)
            m1 = round_trip(m - m0)
            m2 = m - m0 - m1
            t0 = round_trip(t)
            t1 = t - t0
            for n, value in enumerate((m0, m1, m2, t0, t1)):
                stats = jnp.where(lane == 8 * w + n, value, stats)
        halves.append(jnp.concatenate([park_a[2 * half], park_a[2 * half + 1], stats], axis=1))
    a_block = jnp.concatenate(halves, axis=0).astype(BF16)
    a_send[...] = a_block
    a_recv, a_sent = launch(0, NREQ, lambda n: a_send, a_all, a_ss.at[0], a_rs.at[0], ahead)
    a_all[NREQ - 1] = a_block
    q_sent()

    new_score = [SCALE * jnp.sum(q[:, h * HD:(h + 1) * HD] * k[:, h * HD:(h + 1) * HD], axis=1, keepdims=True)
                 for h in range(NHEAD)]

    loads["ids"].wait()
    ids = ids_ref[...]
    expert = iota((E, ROWS), 0)
    chosen_t = jnp.zeros((E, ROWS), F32)
    for n in range(ids.shape[0]):
        chosen_t = jnp.where(ids[n:n + 1] == expert, 1.0, chosen_t)
    before = iota((ROWS, ROWS), 1) < iota((ROWS, ROWS), 0)
    same = iota((ROWS, ROWS), 1) == iota((ROWS, ROWS), 0)
    both = jnp.concatenate([same.astype(F32), before.astype(F32)], axis=0).astype(BF16)
    chosen_rank = lax.dot_general(
        both, chosen_t.astype(BF16), (((1,), (1,)), ((), ())), preferred_element_type=F32)
    chosen = chosen_rank[:ROWS]
    expand = (iota((E, wide), 0) == dst * 2 + (iota((1, wide), 1) % RES) // 4).astype(F32).astype(BF16)
    placed = dot(chosen_rank.astype(BF16), expand)
    taken = jnp.where((placed[:ROWS] > 0.5) & (placed[ROWS:] == (g_col % 4).astype(F32)), 1.0, 0.0)
    low_half = (g_col % ROWS) // RES == 0
    taken_halves = jnp.concatenate([jnp.where(low_half, taken, 0.0), jnp.where(low_half, 0.0, taken)], axis=0)
    taken_t = taken_halves.T.astype(BF16)
    loads["wo"].wait()
    loads["gain_m"].wait()

    a_recv()
    back = dot(hot_home, a_all[...].reshape(wide, 384))
    pieces = []
    for h in range(NHEAD):
        half, w = h // 2, h % 2
        rows = back[half * RES:(half + 1) * RES]
        st = rows[:, 256 + 8 * w:256 + 8 * w + 5]
        back_m = st[:, 0:1] + st[:, 1:2] + st[:, 2:3]
        back_t = st[:, 3:4] + st[:, 4:5]
        a = jnp.concatenate([home_a[h], rows[:, w * HD:(w + 1) * HD]], axis=0)
        m = jnp.concatenate([home_m[h], back_m], axis=0)
        t = jnp.concatenate([home_t[h], back_t], axis=0)
        top = jnp.maximum(m, new_score[h])
        old = t * jnp.exp(m - top)
        new = jnp.exp(new_score[h] - top)
        total = old + new
        pieces.append(a * (old / total) + v[:, h * HD:(h + 1) * HD] * (new / total))
    attended = jnp.concatenate(pieces, axis=1).astype(BF16)

    head_all[head] = dot(attended, wo[...]).astype(BF16)
    h_recv, h_sent = head_exchange(lambda p: head_all.at[head], head_all, h_ss, h_rs)
    a_sent()
    loads["wr"].wait()
    h_recv()
    residual = hidden + ((head_all[0].astype(F32) + head_all[1].astype(F32))
                         + (head_all[2].astype(F32) + head_all[3].astype(F32)))
    normed_f = round_trip(rms_scale(residual, gain_m_ref[...]))

    stacked = jnp.concatenate([normed_f[:, :1024], normed_f[:, 1024:]], axis=0).astype(BF16)
    disp[...] = dot(taken_t, stacked).astype(BF16).reshape(NREQ, ROWS, 1024)
    moves = [launch(lo, hi, lambda n: disp.at[n], arrived, d_ss.at[g], d_rs.at[g], ahead)
             for g, (lo, hi) in enumerate(GROUPS)]
    arrived[NREQ - 1] = disp[NREQ - 1]
    resid[...] = residual
    h_sent()

    logits = lax.dot_general(
        normed_f.astype(BF16), wr[...], (((1,), (1,)), ((), ())), preferred_element_type=F32)
    hit = chosen > 0.5
    top = jnp.max(jnp.where(hit, logits, -3e38), axis=1, keepdims=True)
    power = jnp.where(hit, jnp.exp(jnp.where(hit, logits, top) - top), 0.0)
    gates = power / jnp.sum(power, axis=1, keepdims=True)
    g_hi = round_trip(gates)
    gate_wide = dot(jnp.concatenate([g_hi, gates - g_hi], axis=0).astype(BF16), expand)
    mix_hi = gate_wide[:ROWS] * taken
    mix_lo = gate_wide[ROWS:] * taken
    mix = jnp.concatenate([
        jnp.where(low_half, mix_hi, 0.0), jnp.where(low_half, mix_lo, 0.0),
        jnp.where(low_half, 0.0, mix_hi), jnp.where(low_half, 0.0, mix_lo)], axis=0).astype(BF16)

    loads["wg"].wait()
    loads["wu"].wait()
    loads["wd"].wait()
    returns = []
    for g, (lo, hi) in enumerate(GROUPS):
        moves[g][0]()
        count = hi - lo
        tokens = arrived[lo:hi].astype(F32).reshape(count, 2, RES, 1024)
        left = tokens[:, 0].reshape(count * RES, 1024).astype(BF16)
        right = tokens[:, 1].reshape(count * RES, 1024).astype(BF16)
        which = (iota((count * RES, FFL), 0) % RES) // 4
        inner = []
        for e in range(2):
            gate = dot(left, wg[e, :1024]) + dot(right, wg[e, 1024:])
            up = dot(left, wu[e, :1024]) + dot(right, wu[e, 1024:])
            act = gate / (1.0 + jnp.exp(-gate)) * up
            inner.append(jnp.where(which == e, act, 0.0).astype(BF16))
        parts = []
        for half in range(2):
            cols = slice(half * 1024, (half + 1) * 1024)
            y = dot(inner[0], wd[0, :, cols]) + dot(inner[1], wd[1, :, cols])
            parts.append(y.reshape(count, RES, 1024))
        ret_send[lo:hi] = jnp.concatenate(parts, axis=1).astype(BF16)
        returns.append(launch(lo, hi, lambda n: ret_send.at[n], ret, r_ss.at[g], r_rs.at[g], behind))
    ret[NREQ - 1] = ret_send[NREQ - 1]
    for move in moves:
        move[1]()
    for back_move in returns:
        back_move[0]()
    mixed = dot(mix, ret[...].reshape(wide, 1024))
    mixture = [mixed[0:16] + mixed[16:32], mixed[32:48] + mixed[48:64]]
    for h in range(NHEAD):
        fin_send[h] = mixture[h // 2][:, (h % 2) * WIDTH:(h % 2 + 1) * WIDTH].astype(BF16)
    f_recv, f_sent = head_exchange(lambda p: fin_send.at[p], fin_all, f_ss, f_rs)
    fin_all[head] = fin_send[head]
    for back_move in returns:
        back_move[1]()
    own = resid[:, pl.ds(pl.multiple_of(head * WIDTH, WIDTH), WIDTH)]
    f_recv()
    total = own + ((fin_all[0].astype(F32) + fin_all[1].astype(F32))
                   + (fin_all[2].astype(F32) + fin_all[3].astype(F32)))
    out_ref[...] = total.astype(BF16)
    f_sent()


def body(hidden_in, gain_attn, gain_moe, w_query, w_key, w_value, w_out, w_router, w_gate, w_up, w_down,
         cache_kv, parked_kv, lengths, cache_source, expert_ids):
    half = HD // 2
    freq = 50000.0 ** (-2.0 * np.arange(half, dtype=np.float64) / HD)
    table = np.zeros((8, NREQ * ROWS), np.float32)
    table[0, :HD] = np.concatenate([freq, freq])
    table[1:4] = np.repeat(np.asarray(OFFSETS).T, ROWS, axis=1)
    hbm = pl.BlockSpec(memory_space=pl.ANY)
    dma = pltpu.SemaphoreType.DMA
    operands = [hidden_in, gain_attn.reshape(1, D), gain_moe.reshape(1, D), jnp.asarray(table),
                lengths.reshape(1, -1), cache_source.reshape(1, -1), expert_ids.T,
                w_query, w_key, w_value, w_out, w_router.T, w_gate, w_up, w_down, cache_kv, parked_kv]
    q_block = (NREQ, ROWS, 256)
    a_block = (NREQ, ROWS, 384)
    wide = (NREQ, ROWS, 1024)
    return pl.pallas_call(
        kernel,
        out_shape=jax.ShapeDtypeStruct((ROWS, WIDTH), BF16),
        in_specs=[hbm] * len(operands),
        out_specs=pl.BlockSpec(memory_space=pltpu.VMEM),
        scratch_shapes=[pltpu.VMEM(x.shape, x.dtype) for x in operands] + [
            pltpu.VMEM(q_block[1:], BF16), pltpu.VMEM(q_block, BF16),
            pltpu.VMEM(a_block[1:], BF16), pltpu.VMEM(a_block, BF16),
            pltpu.VMEM((NHEAD, ROWS, D), BF16),
            pltpu.VMEM(wide, BF16), pltpu.VMEM(wide, BF16),
            pltpu.VMEM(wide, BF16), pltpu.VMEM(wide, BF16),
            pltpu.VMEM((NHEAD, ROWS, WIDTH), BF16), pltpu.VMEM((NHEAD, ROWS, WIDTH), BF16),
            pltpu.VMEM((ROWS, D), F32),
            dma((len(operands),)),
            dma((1,)), dma((1,)), dma((1,)), dma((1,)),
            dma((NHEAD,)), dma((NHEAD,)),
            dma((len(GROUPS),)), dma((len(GROUPS),)), dma((len(GROUPS),)), dma((len(GROUPS),)),
            dma((NHEAD,)), dma((NHEAD,)),
        ],
        compiler_params=pltpu.CompilerParams(
            collective_id=0, has_side_effects=True, vmem_limit_bytes=60 * 1024 * 1024),
    )(*operands)


def solution(mesh):
    placed = (
        P("req", None),
        P(),
        P(),
        P(None, "head"),
        P(None, "head"),
        P(None, "head"),
        P("head", None),
        P(),
        P("req", None, "head"),
        P("req", None, "head"),
        P("req", "head", None),
        P(None, "req", None, "head"),
        P(None, "req", None, "head"),
        P(),
        P(),
        P("req", None),
    )
    return jax.shard_map(
        body, mesh=mesh, in_specs=placed, out_specs=P("req", "head"), check_vma=False
    )
```

```python
import jax
import jax.numpy as jnp
import numpy as np
from jax import lax
from jax.experimental import pallas as pl
from jax.experimental.pallas import tpu as pltpu
from jax.sharding import PartitionSpec as P

MESH = pl.DeviceIdType.MESH
F32 = jnp.float32
BF16 = jnp.bfloat16
I32 = jnp.int32

D = 2048
HD = 128
E = 64
NREQ = 32
NHEAD = 4
ROWS = 16
RES = 8
SPAN = 256
WIDTH = 512
FFL = 256
SCALE = HD ** (-0.5)


def ring(step):
    return min(step, 4 - step)


OFFSETS = sorted(
    ((dx, dz, dc) for dx in range(4) for dz in range(4) for dc in range(2)),
    key=lambda o: (-(ring(o[0]) + ring(o[1])), -o[2], abs(o[0] - o[1]), o))
GROUPS = ((0, 10), (10, 22), (22, 32))
EPS = 1e-06


def iota(shape, dim):
    return lax.broadcasted_iota(I32, shape, dim)


def rms_scale(x, gain):
    inverse = lax.rsqrt(jnp.mean(x * x, axis=-1, keepdims=True) + EPS)
    return x * inverse * gain


def round_trip(x):
    return x.astype(BF16).astype(F32)


def dot(a, b):
    return jnp.dot(a, b, preferred_element_type=F32)


def rotate(x, cosine, sine):
    parts = []
    for h in range(NHEAD):
        u = x[:, h * HD:(h + 1) * HD]
        parts.append(u * cosine + pltpu.roll(u, HD // 2, 1) * sine)
    return jnp.concatenate(parts, axis=1)


def cache_attention(q, row_lengths, kv):
    stacked = jnp.concatenate([q] * NHEAD, axis=0)
    row = iota((NHEAD * RES, WIDTH), 0)
    col = iota((NHEAD * RES, WIDTH), 1)
    stacked = jnp.where(row // RES == col // HD, stacked, 0.0)
    scores = jnp.zeros((NHEAD * RES, SPAN), F32)
    for i in range(RES):
        part = jnp.where(row % RES == i, stacked, 0.0).astype(BF16)
        scores = scores + lax.dot_general(
            part, kv[0, i], (((1,), (1,)), ((), ())), preferred_element_type=F32)
    scores = scores * SCALE
    limit = jnp.concatenate([row_lengths] * NHEAD, axis=0)
    usable = iota((NHEAD * RES, SPAN), 1).astype(F32) < limit
    scores = jnp.where(usable, scores, -1e30)
    row_max = jnp.max(scores, axis=1, keepdims=True)
    weights = jnp.where(usable, jnp.exp(scores - row_max), 0.0)
    row_total = jnp.sum(weights, axis=1, keepdims=True)
    probs = weights.astype(BF16)
    pieces = [jnp.zeros((RES, HD), F32)] * NHEAD
    small = iota((RES, HD), 0)
    for i in range(RES):
        out = dot(probs, kv[1, i])
        for h in range(NHEAD):
            pieces[h] = jnp.where(
                small == i, out[h * RES:(h + 1) * RES, h * HD:(h + 1) * HD], pieces[h])
    maxes = [row_max[h * RES:(h + 1) * RES] for h in range(NHEAD)]
    totals = [row_total[h * RES:(h + 1) * RES] for h in range(NHEAD)]
    normal = [pieces[h] / totals[h] for h in range(NHEAD)]
    return normal, maxes, totals


def kernel(
    hidden_hbm, gain_a_hbm, gain_m_hbm, table_hbm, lengths_hbm, source_hbm, ids_hbm,
    wq_hbm, wk_hbm, wv_hbm, wo_hbm, wr_hbm, wg_hbm, wu_hbm, wd_hbm, cache_hbm, parked_hbm,
    out_ref,
    hidden_ref, gain_a_ref, gain_m_ref, table_ref, lengths_ref, source_ref, ids_ref,
    wq, wk, wv, wo, wr, wg, wu, wd, cache, parked,
    q_send, q_all, a_send, a_all, st_send, st_all, home_all, back_all, disp, arrived, ret_send, ret,
    fin_send, fin_all, resid,
    load_sem, q_ss, q_rs, a_ss, a_rs, h_ss, h_rs, d_ss, d_rs, y_ss, y_rs, r_ss, r_rs, f_ss, f_rs,
):
    me = lax.axis_index("req")
    head = lax.axis_index("head")
    my_x, my_z, my_c = me // 8, (me // 2) % 4, me % 2

    def ahead(n):
        dx, dz, dc = OFFSETS[n]
        return ((my_x + dx) % 4) * 8 + ((my_z + dz) % 4) * 2 + (my_c + dc) % 2

    def behind(n):
        dx, dz, dc = OFFSETS[n]
        return ((my_x + 4 - dx) % 4) * 8 + ((my_z + 4 - dz) % 4) * 2 + (my_c + dc) % 2

    barrier = pltpu.get_barrier_semaphore()
    for n in range(NREQ - 1):
        pl.semaphore_signal(barrier, inc=1, device_id={"req": ahead(n)}, device_id_type=MESH)
    for d in range(1, NHEAD):
        pl.semaphore_signal(barrier, inc=1, device_id={"head": (head + d) % NHEAD}, device_id_type=MESH)

    loads = {}
    order = [("hidden", hidden_hbm, hidden_ref), ("gain_a", gain_a_hbm, gain_a_ref),
             ("table", table_hbm, table_ref), ("lengths", lengths_hbm, lengths_ref),
             ("wq", wq_hbm, wq), ("source", source_hbm, source_ref), ("ids", ids_hbm, ids_ref),
             ("gain_m", gain_m_hbm, gain_m_ref),
             ("wk", wk_hbm, wk), ("wv", wv_hbm, wv), ("cache", cache_hbm, cache),
             ("parked", parked_hbm, parked), ("wo", wo_hbm, wo), ("wr", wr_hbm, wr),
             ("wg", wg_hbm, wg), ("wu", wu_hbm, wu), ("wd", wd_hbm, wd)]
    for n, (name, src, dst) in enumerate(order):
        loads[name] = pltpu.make_async_copy(src, dst, load_sem.at[n])
        loads[name].start()

    def launch(lo, hi, source, landing, ss, rs, target):
        hi = min(hi, NREQ - 1)
        for n in range(lo, hi):
            pltpu.make_async_remote_copy(
                src_ref=source(n), dst_ref=landing(n), send_sem=ss, recv_sem=rs,
                device_id={"req": target(n)}, device_id_type=MESH).start()
        span = landing(pl.ds(lo, hi - lo))
        whole = pltpu.make_async_remote_copy(
            src_ref=span, dst_ref=span, send_sem=ss, recv_sem=rs,
            device_id={"req": target(lo)}, device_id_type=MESH)
        return whole.wait_recv, whole.wait_send

    def head_exchange(source, landing, ss, rs):
        def copy(d, own):
            peer = (head + d) % NHEAD
            return pltpu.make_async_remote_copy(
                src_ref=source(peer), dst_ref=landing(head if own else peer), send_sem=ss.at[d],
                recv_sem=rs.at[head if own else peer], device_id={"head": peer}, device_id_type=MESH)

        for d in range(1, NHEAD):
            copy(d, True).start()

        def received():
            for d in range(1, NHEAD):
                copy(d, False).wait_recv()

        def sent():
            for d in range(1, NHEAD):
                copy(d, True).wait_send()

        return received, sent

    for name in ("hidden", "gain_a", "table", "lengths"):
        loads[name].wait()
    hidden = hidden_ref[...].astype(F32)
    normed = rms_scale(hidden, gain_a_ref[...]).astype(BF16)
    pick = iota((ROWS, NREQ * ROWS), 1) == me * ROWS + iota((ROWS, NREQ * ROWS), 0)
    lengths = lengths_ref[...].astype(F32)
    own_len = jnp.sum(jnp.where(pick, lengths, 0.0), axis=1, keepdims=True)
    angles = own_len * table_ref[0:1, :HD]
    cosine = jnp.cos(angles)
    sine = jnp.sin(angles)
    sine = jnp.where(iota((ROWS, HD), 1) < HD // 2, -sine, sine)
    loads["wq"].wait()
    q = round_trip(rotate(dot(normed, wq[...]), cosine, sine))
    q_block = jnp.concatenate([q[RES:, :256], q[RES:, 256:]], axis=0).astype(BF16)
    q_send[...] = q_block
    q_all[NREQ - 1] = q_block

    wide = NREQ * ROWS
    g_row = iota((ROWS, wide), 0)
    g_col = iota((ROWS, wide), 1)
    same_half = g_row // RES == (g_col % ROWS) // RES
    step_x = table_ref[1:2, :].astype(I32)
    step_z = table_ref[2:3, :].astype(I32)
    step_c = table_ref[3:4, :].astype(I32)
    src = ((my_x + 4 - step_x) % 4) * 8 + ((my_z + 4 - step_z) % 4) * 2 + (my_c + step_c) % 2
    dst = ((my_x + step_x) % 4) * 8 + ((my_z + step_z) % 4) * 2 + (my_c + step_c) % 2
    place = src * RES + iota((1, wide), 1) % RES
    natural = iota((256, wide), 1)
    spread = jnp.concatenate([
        (iota((256, wide), 0) == place).astype(F32),
        ((iota((256, wide), 0) == (natural // ROWS) * RES + natural % RES)
         & (natural % ROWS >= RES)).astype(F32)], axis=1).astype(BF16)
    loads["source"].wait()
    source = source_ref[...].astype(F32)
    source_wide = dot(jnp.broadcast_to(source, (RES, 256)).astype(BF16), spread)[0:1]
    hot_park = (same_half & (source_wide[:, :wide] == (me * RES + g_row % RES).astype(F32))).astype(F32).astype(BF16)
    row8 = iota((RES, wide), 0)
    hot_len = (source_wide[:, wide:] == (me * RES + row8).astype(F32)) & (iota((RES, wide), 1) % ROWS >= RES)
    park_len = jnp.sum(jnp.where(hot_len, lengths, 0.0), axis=1, keepdims=True)
    pick = iota((ROWS, 256), 1) == me * RES + iota((ROWS, 256), 0) % RES
    own_source = jnp.sum(jnp.where(pick, source, 0.0), axis=1, keepdims=True)
    block_src = table_ref[4:7, :3 * NREQ].astype(I32)
    block_src = (((my_x + 4 - block_src[0:1]) % 4) * 8 + ((my_z + 4 - block_src[1:2]) % 4) * 2
                 + (my_c + block_src[2:3]) % 2)
    hot_block = (jnp.floor(own_source[:RES] / RES) == block_src.astype(F32)).astype(F32).astype(BF16)
    hot_home = (same_half & (own_source == place.astype(F32))).astype(F32).astype(BF16)

    pl.semaphore_wait(barrier, NREQ - 1 + NHEAD - 1)
    q_recv, q_sent = launch(0, NREQ, lambda n: q_send, lambda n: q_all.at[n], q_ss.at[0], q_rs.at[0], ahead)

    loads["wk"].wait()
    k = round_trip(rotate(dot(normed, wk[...]), cosine, sine))
    loads["wv"].wait()
    v = round_trip(dot(normed, wv[...]))
    loads["cache"].wait()
    home_a, home_m, home_t = cache_attention(q[:RES], own_len[:RES], cache)
    loads["parked"].wait()

    q_recv()
    parked_q = dot(hot_park, q_all[...].reshape(wide, 256))
    park_a, park_m, park_t = cache_attention(
        jnp.concatenate([parked_q[:RES], parked_q[RES:]], axis=1), park_len, parked)

    a_block = jnp.concatenate([
        jnp.concatenate(park_a[:2], axis=1), jnp.concatenate(park_a[2:], axis=1)], axis=0).astype(BF16)
    a_send[...] = a_block
    a_recv, a_sent = launch(0, NREQ, lambda n: a_send, lambda n: a_all.at[n], a_ss.at[0], a_rs.at[0], ahead)
    stats = jnp.concatenate(park_m + park_t, axis=0)
    shape = (2 * NHEAD * RES, HD)
    stats = jnp.sum(jnp.where(iota(shape, 0) == iota(shape, 1), stats, 0.0), axis=0, keepdims=True)
    st_send[...] = stats
    st_recv, st_sent = launch(0, NREQ, lambda n: st_send, lambda n: st_all.at[n], a_ss.at[1], a_rs.at[1], ahead)
    a_all[NREQ - 1] = a_block
    st_all[NREQ - 1] = stats
    q_sent()

    new_score = [SCALE * jnp.sum(q[:, h * HD:(h + 1) * HD] * k[:, h * HD:(h + 1) * HD], axis=1, keepdims=True)
                 for h in range(NHEAD)]

    def finish(first, a, m, t):
        pieces = []
        for h in range(NHEAD):
            score = new_score[h][first:first + RES]
            top = jnp.maximum(m[h], score)
            old = t[h] * jnp.exp(m[h] - top)
            new = jnp.exp(score - top)
            total = old + new
            pieces.append(a[h] * (old / total) + v[first:first + RES, h * HD:(h + 1) * HD] * (new / total))
        out = dot(jnp.concatenate(pieces, axis=1).astype(BF16), wo[...])
        return jnp.concatenate([out[:, :1024], out[:, 1024:]], axis=0).astype(BF16)

    def summed(parts):
        whole = (parts[0].astype(F32) + parts[1].astype(F32)) + (parts[2].astype(F32) + parts[3].astype(F32))
        return jnp.concatenate([whole[:RES], whole[RES:]], axis=1)

    loads["wo"].wait()
    home_all[head] = finish(0, home_a, home_m, home_t)
    home_recv, home_sent = head_exchange(lambda p: home_all.at[head], lambda p: home_all.at[p], h_ss.at[0], h_rs.at[0])

    loads["ids"].wait()
    ids = ids_ref[...]
    expert = iota((E, ROWS), 0)
    chosen_t = jnp.zeros((E, ROWS), F32)
    for n in range(ids.shape[0]):
        chosen_t = jnp.where(ids[n:n + 1] == expert, 1.0, chosen_t)
    before = iota((ROWS, ROWS), 1) < iota((ROWS, ROWS), 0)
    same = iota((ROWS, ROWS), 1) == iota((ROWS, ROWS), 0)
    both = jnp.concatenate([same.astype(F32), before.astype(F32)], axis=0).astype(BF16)
    chosen_rank = lax.dot_general(
        both, chosen_t.astype(BF16), (((1,), (1,)), ((), ())), preferred_element_type=F32)
    chosen = chosen_rank[:ROWS]
    expand = (iota((E, wide), 0) == dst * 2 + (iota((1, wide), 1) % RES) // 4).astype(F32).astype(BF16)
    placed = dot(chosen_rank.astype(BF16), expand)
    taken = jnp.where((placed[:ROWS] > 0.5) & (placed[ROWS:] == (g_col % 4).astype(F32)), 1.0, 0.0)
    low_half = (g_col % ROWS) // RES == 0
    taken_halves = jnp.concatenate([jnp.where(low_half, taken, 0.0), jnp.where(low_half, 0.0, taken)], axis=0)
    taken_t = taken_halves.T.astype(BF16)
    loads["gain_m"].wait()
    home_recv()
    home_residual = hidden[:RES] + summed(home_all)

    a_recv()
    back = dot(hot_home, a_all[...].reshape(wide, 256))
    st_recv()
    st = st_all[...].reshape(NREQ, HD)
    st0 = round_trip(st)
    st1 = round_trip(st - st0)
    st = jnp.concatenate([st0, st1, st - st0 - st1], axis=0).astype(BF16)
    picked = dot(hot_block, st)
    lane = iota((RES, HD), 1).astype(F32)
    turn = own_source[:RES] - jnp.floor(own_source[:RES] / RES) * RES
    back_s = [jnp.sum(jnp.where(lane == turn + n * RES, picked, 0.0), axis=1, keepdims=True)
              for n in range(2 * NHEAD)]
    back_a = [back[(h // 2) * RES:(h // 2 + 1) * RES, (h % 2) * HD:(h % 2 + 1) * HD] for h in range(NHEAD)]
    back_all[head] = finish(RES, back_a, back_s[:NHEAD], back_s[NHEAD:])
    h_recv, h_sent = head_exchange(lambda p: back_all.at[head], lambda p: back_all.at[p], h_ss.at[1], h_rs.at[1])
    a_sent()
    st_sent()
    home_sent()
    loads["wr"].wait()
    h_recv()
    residual = jnp.concatenate([home_residual, hidden[RES:] + summed(back_all)], axis=0)
    normed_f = round_trip(rms_scale(residual, gain_m_ref[...]))

    stacked = jnp.concatenate([normed_f[:, :1024], normed_f[:, 1024:]], axis=0).astype(BF16)
    disp[...] = dot(taken_t, stacked).astype(BF16).reshape(NREQ, ROWS, 1024)
    def quarter(p):
        return pl.ds(pl.multiple_of(p * 256, 256), 256)

    far = GROUPS[0][1]
    moves = [launch(0, far, lambda n: disp.at[n, :, quarter(head)], lambda n: arrived.at[n, :, quarter(head)],
                    d_ss.at[0], d_rs.at[0], ahead)]
    for g, (lo, hi) in list(enumerate(GROUPS))[1:]:
        moves.append(launch(lo, hi, lambda n: disp.at[n], lambda n: arrived.at[n], d_ss.at[g], d_rs.at[g], ahead))
    arrived[NREQ - 1] = disp[NREQ - 1]
    resid[...] = residual
    h_sent()

    logits = lax.dot_general(
        normed_f.astype(BF16), wr[...], (((1,), (1,)), ((), ())), preferred_element_type=F32)
    hit = chosen > 0.5
    top = jnp.max(jnp.where(hit, logits, -3e38), axis=1, keepdims=True)
    power = jnp.where(hit, jnp.exp(jnp.where(hit, logits, top) - top), 0.0)
    gates = power / jnp.sum(power, axis=1, keepdims=True)
    g_hi = round_trip(gates)
    gate_wide = dot(jnp.concatenate([g_hi, gates - g_hi], axis=0).astype(BF16), expand)
    mix_hi = gate_wide[:ROWS] * taken
    mix_lo = gate_wide[ROWS:] * taken
    mix = jnp.concatenate([
        jnp.where(low_half, mix_hi, 0.0), jnp.where(low_half, mix_lo, 0.0),
        jnp.where(low_half, 0.0, mix_hi), jnp.where(low_half, 0.0, mix_lo)], axis=0).astype(BF16)

    loads["wg"].wait()
    loads["wu"].wait()
    loads["wd"].wait()
    def experts(lo, hi):
        count = hi - lo
        tokens = arrived[lo:hi].astype(F32).reshape(count, 2, RES, 1024)
        left = tokens[:, 0].reshape(count * RES, 1024).astype(BF16)
        right = tokens[:, 1].reshape(count * RES, 1024).astype(BF16)
        which = (iota((count * RES, FFL), 0) % RES) // 4
        inner = []
        for e in range(2):
            gate = dot(left, wg[e, :1024]) + dot(right, wg[e, 1024:])
            up = dot(left, wu[e, :1024]) + dot(right, wu[e, 1024:])
            act = gate / (1.0 + jnp.exp(-gate)) * up
            inner.append(jnp.where(which == e, act, 0.0).astype(BF16))
        parts = []
        for half in range(2):
            cols = slice(half * 1024, (half + 1) * 1024)
            y = dot(inner[0], wd[0, :, cols]) + dot(inner[1], wd[1, :, cols])
            parts.append(y.reshape(count, RES, 1024))
        ret_send[lo:hi] = jnp.concatenate(parts, axis=1).astype(BF16)

    def give_back(g):
        lo, hi = GROUPS[g]
        return launch(lo, hi, lambda n: ret_send.at[n], lambda n: ret.at[n], r_ss.at[g], r_rs.at[g], behind)

    moves[0][0]()
    y_recv, y_sent = head_exchange(
        lambda p: arrived.at[pl.ds(0, far), :, quarter(head)],
        lambda p: arrived.at[pl.ds(0, far), :, quarter(p)], y_ss, y_rs)
    moves[1][0]()
    experts(*GROUPS[1])
    returns = [give_back(1)]
    moves[2][0]()
    experts(*GROUPS[2])
    ret[NREQ - 1] = ret_send[NREQ - 1]
    y_recv()
    experts(*GROUPS[0])
    returns.append(give_back(0))
    returns.append(give_back(2))
    y_sent()
    for move in moves:
        move[1]()
    for back_move in returns:
        back_move[0]()
    mixed = dot(mix, ret[...].reshape(wide, 1024))
    mixture = [mixed[0:16] + mixed[16:32], mixed[32:48] + mixed[48:64]]
    for h in range(NHEAD):
        fin_send[h] = mixture[h // 2][:, (h % 2) * WIDTH:(h % 2 + 1) * WIDTH].astype(BF16)
    f_recv, f_sent = head_exchange(lambda p: fin_send.at[p], lambda p: fin_all.at[p], f_ss, f_rs)
    fin_all[head] = fin_send[head]
    for back_move in returns:
        back_move[1]()
    own = resid[:, pl.ds(pl.multiple_of(head * WIDTH, WIDTH), WIDTH)]
    f_recv()
    total = own + ((fin_all[0].astype(F32) + fin_all[1].astype(F32))
                   + (fin_all[2].astype(F32) + fin_all[3].astype(F32)))
    out_ref[...] = total.astype(BF16)
    f_sent()


def body(hidden_in, gain_attn, gain_moe, w_query, w_key, w_value, w_out, w_router, w_gate, w_up, w_down,
         cache_kv, parked_kv, lengths, cache_source, expert_ids):
    half = HD // 2
    freq = 50000.0 ** (-2.0 * np.arange(half, dtype=np.float64) / HD)
    table = np.zeros((8, NREQ * ROWS), np.float32)
    table[0, :HD] = np.concatenate([freq, freq])
    table[1:4] = np.repeat(np.asarray(OFFSETS).T, ROWS, axis=1)
    table[4:7, :3 * NREQ] = np.tile(np.asarray(OFFSETS).T, (1, 3))
    hbm = pl.BlockSpec(memory_space=pl.ANY)
    dma = pltpu.SemaphoreType.DMA
    operands = [hidden_in, gain_attn.reshape(1, D), gain_moe.reshape(1, D), jnp.asarray(table),
                lengths.reshape(1, -1), cache_source.reshape(1, -1), expert_ids.T,
                w_query, w_key, w_value, w_out, w_router.T, w_gate, w_up, w_down, cache_kv, parked_kv]
    q_block = (NREQ, ROWS, 256)
    wide = (NREQ, ROWS, 1024)
    return pl.pallas_call(
        kernel,
        out_shape=jax.ShapeDtypeStruct((ROWS, WIDTH), BF16),
        in_specs=[hbm] * len(operands),
        out_specs=pl.BlockSpec(memory_space=pltpu.VMEM),
        scratch_shapes=[pltpu.VMEM(x.shape, x.dtype) for x in operands] + [
            pltpu.VMEM(q_block[1:], BF16), pltpu.VMEM(q_block, BF16),
            pltpu.VMEM(q_block[1:], BF16), pltpu.VMEM(q_block, BF16),
            pltpu.VMEM((1, HD), F32), pltpu.VMEM((NREQ, 1, HD), F32),
            pltpu.VMEM((NHEAD, ROWS, 1024), BF16), pltpu.VMEM((NHEAD, ROWS, 1024), BF16),
            pltpu.VMEM(wide, BF16), pltpu.VMEM(wide, BF16),
            pltpu.VMEM(wide, BF16), pltpu.VMEM(wide, BF16),
            pltpu.VMEM((NHEAD, ROWS, WIDTH), BF16), pltpu.VMEM((NHEAD, ROWS, WIDTH), BF16),
            pltpu.VMEM((ROWS, D), F32),
            dma((len(operands),)),
            dma((1,)), dma((1,)), dma((2,)), dma((2,)),
            dma((2, NHEAD)), dma((2, NHEAD)),
            dma((len(GROUPS),)), dma((len(GROUPS),)), dma((NHEAD,)), dma((NHEAD,)),
            dma((len(GROUPS),)), dma((len(GROUPS),)),
            dma((NHEAD,)), dma((NHEAD,)),
        ],
        compiler_params=pltpu.CompilerParams(
            collective_id=0, has_side_effects=True, vmem_limit_bytes=60 * 1024 * 1024),
    )(*operands)


def solution(mesh):
    placed = (
        P("req", None),
        P(),
        P(),
        P(None, "head"),
        P(None, "head"),
        P(None, "head"),
        P("head", None),
        P(),
        P("req", None, "head"),
        P("req", None, "head"),
        P("req", "head", None),
        P(None, "req", None, "head"),
        P(None, "req", None, "head"),
        P(),
        P(),
        P("req", None),
    )
    return jax.shard_map(
        body, mesh=mesh, in_specs=placed, out_specs=P("req", "head"), check_vma=False
    )
```

```python
import jax
import jax.numpy as jnp
import numpy as np
from jax import lax
from jax.experimental import pallas as pl
from jax.experimental.pallas import tpu as pltpu
from jax.sharding import PartitionSpec as P

MESH = pl.DeviceIdType.MESH
F32 = jnp.float32
BF16 = jnp.bfloat16
I32 = jnp.int32

D = 2048
HD = 128
E = 64
NREQ = 32
NHEAD = 4
ROWS = 16
RES = 8
SPAN = 256
WIDTH = 512
FFL = 256
SCALE = HD ** (-0.5)


def ring(step):
    return min(step, 4 - step)


OFFSETS = sorted(
    ((dx, dz, dc) for dx in range(4) for dz in range(4) for dc in range(2)),
    key=lambda o: (-(ring(o[0]) + ring(o[1])), -o[2], abs(o[0] - o[1]), o))
FAR = ((0, 6), (6, 10))
NEAR = ((10, 22), (22, 32))
FIRST = 10
EPS = 1e-06


def iota(shape, dim):
    return lax.broadcasted_iota(I32, shape, dim)


def rms_scale(x, gain):
    inverse = lax.rsqrt(jnp.mean(x * x, axis=-1, keepdims=True) + EPS)
    return x * inverse * gain


def round_trip(x):
    return x.astype(BF16).astype(F32)


def dot(a, b):
    return jnp.dot(a, b, preferred_element_type=F32)


def split(x):
    blocks = [x[:, n * 256:(n + 1) * 256] for n in range(8)]
    return jnp.concatenate(blocks[::2], axis=1), jnp.concatenate(blocks[1::2], axis=1)


def join(even, odd):
    width = even.shape[1] // 256
    return jnp.concatenate(
        [part[:, n * 256:(n + 1) * 256] for n in range(width) for part in (even, odd)], axis=1)


def rotate(x, cosine, sine):
    parts = []
    for h in range(NHEAD):
        u = x[:, h * HD:(h + 1) * HD]
        parts.append(u * cosine + pltpu.roll(u, HD // 2, 1) * sine)
    return jnp.concatenate(parts, axis=1)


def cache_attention(q, row_lengths, kv):
    stacked = jnp.concatenate([q] * NHEAD, axis=0)
    row = iota((NHEAD * RES, WIDTH), 0)
    col = iota((NHEAD * RES, WIDTH), 1)
    stacked = jnp.where(row // RES == col // HD, stacked, 0.0)
    scores = jnp.zeros((NHEAD * RES, SPAN), F32)
    for i in range(RES):
        part = jnp.where(row % RES == i, stacked, 0.0).astype(BF16)
        scores = scores + lax.dot_general(
            part, kv[0, i], (((1,), (1,)), ((), ())), preferred_element_type=F32)
    scores = scores * SCALE
    limit = jnp.concatenate([row_lengths] * NHEAD, axis=0)
    usable = iota((NHEAD * RES, SPAN), 1).astype(F32) < limit
    scores = jnp.where(usable, scores, -1e30)
    row_max = jnp.max(scores, axis=1, keepdims=True)
    weights = jnp.where(usable, jnp.exp(scores - row_max), 0.0)
    row_total = jnp.sum(weights, axis=1, keepdims=True)
    probs = weights.astype(BF16)
    pieces = [jnp.zeros((RES, HD), F32)] * NHEAD
    small = iota((RES, HD), 0)
    for i in range(RES):
        out = dot(probs, kv[1, i])
        for h in range(NHEAD):
            pieces[h] = jnp.where(
                small == i, out[h * RES:(h + 1) * RES, h * HD:(h + 1) * HD], pieces[h])
    maxes = [row_max[h * RES:(h + 1) * RES] for h in range(NHEAD)]
    totals = [row_total[h * RES:(h + 1) * RES] for h in range(NHEAD)]
    normal = [pieces[h] / totals[h] for h in range(NHEAD)]
    return normal, maxes, totals


def kernel(
    hidden_hbm, gain_a_hbm, gain_m_hbm, table_hbm, lengths_hbm, source_hbm, ids_hbm,
    wq_hbm, wk_hbm, wv_hbm, wo_hbm, wr_hbm, wg_hbm, wu_hbm, wd_hbm, cache_hbm, parked_hbm,
    out_ref,
    hidden_ref, gain_a_ref, gain_m_ref, table_ref, lengths_ref, source_ref, ids_ref,
    wq, wk, wv, wo, wr, wg, wu, wd, cache, parked,
    q_send, q_all, a_send, a_all, st_send, st_all, home_all, back_all, disp, arrived, ret_send, ret,
    part_all, far_send, far_ret, fin_send, fin_all, resid,
    load_sem, q_ss, q_rs, a_ss, a_rs, h_ss, h_rs, d_ss, d_rs, y_ss, y_rs, p_ss, p_rs, t_ss, t_rs,
    r_ss, r_rs, f_ss, f_rs,
):
    me = lax.axis_index("req")
    head = lax.axis_index("head")
    my_x, my_z, my_c = me // 8, (me // 2) % 4, me % 2

    def ahead(n):
        dx, dz, dc = OFFSETS[n]
        return ((my_x + dx) % 4) * 8 + ((my_z + dz) % 4) * 2 + (my_c + dc) % 2

    def behind(n):
        dx, dz, dc = OFFSETS[n]
        return ((my_x + 4 - dx) % 4) * 8 + ((my_z + 4 - dz) % 4) * 2 + (my_c + dc) % 2

    barrier = pltpu.get_barrier_semaphore()
    for n in range(NREQ - 1):
        pl.semaphore_signal(barrier, inc=1, device_id={"req": ahead(n)}, device_id_type=MESH)
    for d in range(1, NHEAD):
        pl.semaphore_signal(barrier, inc=1, device_id={"head": (head + d) % NHEAD}, device_id_type=MESH)

    loads = {}
    order = [("hidden", hidden_hbm, hidden_ref), ("gain_a", gain_a_hbm, gain_a_ref),
             ("table", table_hbm, table_ref), ("lengths", lengths_hbm, lengths_ref),
             ("wq", wq_hbm, wq), ("source", source_hbm, source_ref), ("ids", ids_hbm, ids_ref),
             ("gain_m", gain_m_hbm, gain_m_ref),
             ("wk", wk_hbm, wk), ("wv", wv_hbm, wv), ("cache", cache_hbm, cache),
             ("parked", parked_hbm, parked), ("wo", wo_hbm, wo), ("wr", wr_hbm, wr),
             ("wg", wg_hbm, wg), ("wu", wu_hbm, wu), ("wd", wd_hbm, wd)]
    for n, (name, src, dst) in enumerate(order):
        loads[name] = pltpu.make_async_copy(src, dst, load_sem.at[n])
        loads[name].start()

    def launch(lo, hi, source, landing, ss, rs, target):
        hi = min(hi, NREQ - 1)
        for n in range(lo, hi):
            pltpu.make_async_remote_copy(
                src_ref=source(n), dst_ref=landing(n), send_sem=ss, recv_sem=rs,
                device_id={"req": target(n)}, device_id_type=MESH).start()
        span = landing(pl.ds(lo, hi - lo))
        whole = pltpu.make_async_remote_copy(
            src_ref=span, dst_ref=span, send_sem=ss, recv_sem=rs,
            device_id={"req": target(lo)}, device_id_type=MESH)
        return whole.wait_recv, whole.wait_send

    def head_exchange(source, landing, ss, rs):
        def copy(d, own):
            peer = (head + d) % NHEAD
            return pltpu.make_async_remote_copy(
                src_ref=source(peer), dst_ref=landing(head if own else peer), send_sem=ss.at[d],
                recv_sem=rs.at[head if own else peer], device_id={"head": peer}, device_id_type=MESH)

        mine = [copy(d, True) for d in range(1, NHEAD)]
        theirs = [copy(d, False) for d in range(1, NHEAD)]
        for move in mine:
            move.start()
        return (lambda: [move.wait_recv() for move in theirs]), (lambda: [move.wait_send() for move in mine])

    for name in ("hidden", "gain_a", "table", "lengths"):
        loads[name].wait()
    hidden = hidden_ref[...].astype(F32)
    normed = rms_scale(hidden, gain_a_ref[...]).astype(BF16)
    pick = iota((ROWS, NREQ * ROWS), 1) == me * ROWS + iota((ROWS, NREQ * ROWS), 0)
    lengths = lengths_ref[...].astype(F32)
    own_len = jnp.sum(jnp.where(pick, lengths, 0.0), axis=1, keepdims=True)
    angles = own_len * table_ref[0:1, :HD]
    cosine = jnp.cos(angles)
    sine = jnp.sin(angles)
    sine = jnp.where(iota((ROWS, HD), 1) < HD // 2, -sine, sine)
    loads["wq"].wait()
    q = round_trip(rotate(dot(normed, wq[...]), cosine, sine))
    q_block = jnp.concatenate([q[RES:, :256], q[RES:, 256:]], axis=0).astype(BF16)
    q_send[...] = q_block
    q_all[NREQ - 1] = q_block

    wide = NREQ * ROWS
    g_row = iota((ROWS, wide), 0)
    g_col = iota((ROWS, wide), 1)
    same_half = g_row // RES == (g_col % ROWS) // RES
    step_x = table_ref[1:2, :].astype(I32)
    step_z = table_ref[2:3, :].astype(I32)
    step_c = table_ref[3:4, :].astype(I32)
    src = ((my_x + 4 - step_x) % 4) * 8 + ((my_z + 4 - step_z) % 4) * 2 + (my_c + step_c) % 2
    dst = ((my_x + step_x) % 4) * 8 + ((my_z + step_z) % 4) * 2 + (my_c + step_c) % 2
    place = src * RES + iota((1, wide), 1) % RES
    natural = iota((256, wide), 1)
    spread = jnp.concatenate([
        (iota((256, wide), 0) == place).astype(F32),
        ((iota((256, wide), 0) == (natural // ROWS) * RES + natural % RES)
         & (natural % ROWS >= RES)).astype(F32)], axis=1).astype(BF16)
    loads["source"].wait()
    source = source_ref[...].astype(F32)
    source_wide = dot(jnp.broadcast_to(source, (RES, 256)).astype(BF16), spread)[0:1]
    hot_park = (same_half & (source_wide[:, :wide] == (me * RES + g_row % RES).astype(F32))).astype(F32).astype(BF16)
    row8 = iota((RES, wide), 0)
    hot_len = (source_wide[:, wide:] == (me * RES + row8).astype(F32)) & (iota((RES, wide), 1) % ROWS >= RES)
    park_len = jnp.sum(jnp.where(hot_len, lengths, 0.0), axis=1, keepdims=True)
    pick = iota((ROWS, 256), 1) == me * RES + iota((ROWS, 256), 0) % RES
    own_source = jnp.sum(jnp.where(pick, source, 0.0), axis=1, keepdims=True)
    block_src = table_ref[4:7, :3 * NREQ].astype(I32)
    block_src = (((my_x + 4 - block_src[0:1]) % 4) * 8 + ((my_z + 4 - block_src[1:2]) % 4) * 2
                 + (my_c + block_src[2:3]) % 2)
    hot_block = (jnp.floor(own_source[:RES] / RES) == block_src.astype(F32)).astype(F32).astype(BF16)
    hot_home = (same_half & (own_source == place.astype(F32))).astype(F32).astype(BF16)

    loads["ids"].wait()
    ids = ids_ref[...]
    expert = iota((E, ROWS), 0)
    chosen_t = jnp.zeros((E, ROWS), F32)
    for n in range(ids.shape[0]):
        chosen_t = jnp.where(ids[n:n + 1] == expert, 1.0, chosen_t)
    before = iota((ROWS, ROWS), 1) < iota((ROWS, ROWS), 0)
    same = iota((ROWS, ROWS), 1) == iota((ROWS, ROWS), 0)
    both = jnp.concatenate([same.astype(F32), before.astype(F32)], axis=0).astype(BF16)
    chosen_rank = lax.dot_general(
        both, chosen_t.astype(BF16), (((1,), (1,)), ((), ())), preferred_element_type=F32)
    chosen = chosen_rank[:ROWS]
    expand = (iota((E, wide), 0) == dst * 2 + (iota((1, wide), 1) % RES) // 4).astype(F32).astype(BF16)
    placed = dot(chosen_rank.astype(BF16), expand)
    taken = jnp.where((placed[:ROWS] > 0.5) & (placed[ROWS:] == (g_col % 4).astype(F32)), 1.0, 0.0)
    low_half = (g_col % ROWS) // RES == 0
    taken_halves = jnp.concatenate([jnp.where(low_half, taken, 0.0), jnp.where(low_half, 0.0, taken)], axis=0)
    taken_t = taken_halves.T.astype(BF16)
    pl.semaphore_wait(barrier, NREQ - 1 + NHEAD - 1)
    q_recv, q_sent = launch(0, NREQ, lambda n: q_send, lambda n: q_all.at[n], q_ss.at[0], q_rs.at[0], ahead)

    loads["wk"].wait()
    k = round_trip(rotate(dot(normed, wk[...]), cosine, sine))
    loads["wv"].wait()
    v = round_trip(dot(normed, wv[...]))
    loads["cache"].wait()
    home_a, home_m, home_t = cache_attention(q[:RES], own_len[:RES], cache)
    new_score = [SCALE * jnp.sum(q[:, h * HD:(h + 1) * HD] * k[:, h * HD:(h + 1) * HD], axis=1, keepdims=True)
                 for h in range(NHEAD)]

    def finish(first, a, m, t):
        pieces = []
        for h in range(NHEAD):
            score = new_score[h][first:first + RES]
            top = jnp.maximum(m[h], score)
            old = t[h] * jnp.exp(m[h] - top)
            new = jnp.exp(score - top)
            total = old + new
            pieces.append(a[h] * (old / total) + v[first:first + RES, h * HD:(h + 1) * HD] * (new / total))
        out = dot(jnp.concatenate(pieces, axis=1).astype(BF16), wo[...])
        return jnp.concatenate([out[:, :1024], out[:, 1024:]], axis=0).astype(BF16)

    def summed(parts):
        whole = (parts[0].astype(F32) + parts[1].astype(F32)) + (parts[2].astype(F32) + parts[3].astype(F32))
        return jnp.concatenate([whole[:RES], whole[RES:]], axis=1)

    loads["wo"].wait()
    home_all[head] = finish(0, home_a, home_m, home_t)
    home_recv, home_sent = head_exchange(lambda p: home_all.at[head], lambda p: home_all.at[p], h_ss.at[0], h_rs.at[0])
    loads["parked"].wait()

    q_recv()
    parked_q = dot(hot_park, q_all[...].reshape(wide, 256))
    park_a, park_m, park_t = cache_attention(
        jnp.concatenate([parked_q[:RES], parked_q[RES:]], axis=1), park_len, parked)

    a_block = jnp.concatenate([
        jnp.concatenate(park_a[:2], axis=1), jnp.concatenate(park_a[2:], axis=1)], axis=0).astype(BF16)
    a_send[...] = a_block
    a_recv, a_sent = launch(0, NREQ, lambda n: a_send, lambda n: a_all.at[n], a_ss.at[0], a_rs.at[0], ahead)
    stats = jnp.concatenate(park_m + park_t, axis=0)
    shape = (2 * NHEAD * RES, HD)
    stats = jnp.sum(jnp.where(iota(shape, 0) == iota(shape, 1), stats, 0.0), axis=0, keepdims=True)
    st_send[...] = stats
    st_recv, st_sent = launch(0, NREQ, lambda n: st_send, lambda n: st_all.at[n], a_ss.at[1], a_rs.at[1], ahead)
    a_all[NREQ - 1] = a_block
    st_all[NREQ - 1] = stats
    q_sent()

    loads["gain_m"].wait()
    home_recv()
    home_residual = hidden[:RES] + summed(home_all)

    a_recv()
    back = dot(hot_home, a_all[...].reshape(wide, 256))
    st_recv()
    st = st_all[...].reshape(NREQ, HD)
    st0 = round_trip(st)
    st1 = round_trip(st - st0)
    st = jnp.concatenate([st0, st1, st - st0 - st1], axis=0).astype(BF16)
    picked = dot(hot_block, st)
    lane = iota((RES, HD), 1).astype(F32)
    turn = own_source[:RES] - jnp.floor(own_source[:RES] / RES) * RES
    back_s = [jnp.sum(jnp.where(lane == turn + n * RES, picked, 0.0), axis=1, keepdims=True)
              for n in range(2 * NHEAD)]
    back_a = [back[(h // 2) * RES:(h // 2 + 1) * RES, (h % 2) * HD:(h % 2 + 1) * HD] for h in range(NHEAD)]
    back_all[head] = finish(RES, back_a, back_s[:NHEAD], back_s[NHEAD:])
    h_recv, h_sent = head_exchange(lambda p: back_all.at[head], lambda p: back_all.at[p], h_ss.at[1], h_rs.at[1])
    a_sent()
    st_sent()
    home_sent()
    loads["wr"].wait()
    h_recv()
    residual = jnp.concatenate([home_residual, hidden[RES:] + summed(back_all)], axis=0)
    normed_f = round_trip(rms_scale(residual, gain_m_ref[...]))

    stacked = jnp.concatenate(split(normed_f), axis=0).astype(BF16)
    disp[...] = dot(taken_t, stacked).astype(BF16).reshape(NREQ, ROWS, 1024)
    def quarter(p):
        return pl.ds(pl.multiple_of(p * 256, 256), 256)

    far_moves = [launch(lo, hi, lambda n: disp.at[n, :, quarter(head)], lambda n: arrived.at[n, :, quarter(head)],
                        d_ss.at[g], d_rs.at[g], ahead) for g, (lo, hi) in enumerate(FAR)]
    moves = [launch(lo, hi, lambda n: disp.at[n], lambda n: arrived.at[n], d_ss.at[2 + g], d_rs.at[2 + g], ahead)
             for g, (lo, hi) in enumerate(NEAR)]
    arrived[NREQ - 1] = disp[NREQ - 1]
    resid[...] = residual
    h_sent()

    logits = lax.dot_general(
        normed_f.astype(BF16), wr[...], (((1,), (1,)), ((), ())), preferred_element_type=F32)
    hit = chosen > 0.5
    top = jnp.max(jnp.where(hit, logits, -3e38), axis=1, keepdims=True)
    power = jnp.where(hit, jnp.exp(jnp.where(hit, logits, top) - top), 0.0)
    gates = power / jnp.sum(power, axis=1, keepdims=True)
    g_hi = round_trip(gates)
    gate_wide = dot(jnp.concatenate([g_hi, gates - g_hi], axis=0).astype(BF16), expand)
    mix_hi = gate_wide[:ROWS] * taken
    mix_lo = gate_wide[ROWS:] * taken
    mix = jnp.concatenate([
        jnp.where(low_half, mix_hi, 0.0), jnp.where(low_half, mix_lo, 0.0),
        jnp.where(low_half, 0.0, mix_hi), jnp.where(low_half, 0.0, mix_lo)], axis=0).astype(BF16)

    loads["wg"].wait()
    loads["wu"].wait()
    loads["wd"].wait()
    def experts(lo, hi):
        count = hi - lo
        tokens = arrived[lo:hi].astype(F32).reshape(count, 2, RES, 1024)
        tokens = join(tokens[:, 0].reshape(count * RES, 1024), tokens[:, 1].reshape(count * RES, 1024)).astype(BF16)
        which = (iota((count * RES, FFL), 0) % RES) // 4
        inner = []
        for e in range(2):
            gate = dot(tokens, wg[e])
            up = dot(tokens, wu[e])
            act = gate / (1.0 + jnp.exp(-gate)) * up
            inner.append(jnp.where(which == e, act, 0.0).astype(BF16))
        out = dot(inner[0], wd[0]) + dot(inner[1], wd[1])
        out = [part.reshape(count, RES, 1024) for part in split(out)]
        ret_send[lo:hi] = jnp.concatenate(out, axis=1).astype(BF16)

    def give_back(g):
        lo, hi = NEAR[g]
        return launch(lo, hi, lambda n: ret_send.at[n], lambda n: ret.at[n], r_ss.at[g], r_rs.at[g], behind)

    swaps = []
    for g, (lo, hi) in enumerate(FAR):
        far_moves[g][0]()
        swaps.append(head_exchange(
            lambda p: arrived.at[pl.ds(lo, hi - lo), :, quarter(head)],
            lambda p: arrived.at[pl.ds(lo, hi - lo), :, quarter(p)], y_ss.at[g], y_rs.at[g]))
    returns = []
    for g, (lo, hi) in enumerate(NEAR):
        moves[g][0]()
        experts(lo, hi)
        returns.append(give_back(g))
    ret[NREQ - 1] = ret_send[NREQ - 1]
    parts = []
    for g, (lo, hi) in enumerate(FAR):
        swaps[g][0]()
        experts(lo, hi)
        parts.append(head_exchange(
            lambda p: ret_send.at[pl.ds(lo, hi - lo), :, quarter(p)],
            lambda p: part_all.at[p, pl.ds(lo, hi - lo)], p_ss.at[g], p_rs.at[g]))
        part_all[head, lo:hi] = ret_send[lo:hi, :, quarter(head)]
    far_returns = []
    for g, (lo, hi) in enumerate(FAR):
        parts[g][0]()
        whole = [part_all[h, lo:hi].astype(F32) for h in range(NHEAD)]
        far_send[lo:hi] = ((whole[0] + whole[1]) + (whole[2] + whole[3])).astype(BF16)
        far_returns.append(launch(
            lo, hi, lambda n: far_send.at[n], lambda n: far_ret.at[n], t_ss.at[g], t_rs.at[g], behind))
    for back_move in returns:
        back_move[0]()
    mixed = dot(mix[:, FIRST * ROWS:], ret[FIRST:].reshape(wide - FIRST * ROWS, 1024))
    mixture = join(mixed[0:16] + mixed[16:32], mixed[32:48] + mixed[48:64])
    for h in range(NHEAD):
        fin_send[h] = mixture[:, h * WIDTH:(h + 1) * WIDTH].astype(BF16)
    f_recv, f_sent = head_exchange(lambda p: fin_send.at[p], lambda p: fin_all.at[p], f_ss, f_rs)
    fin_all[head] = fin_send[head]
    for group in swaps + parts + far_moves + moves + returns:
        group[1]()
    own = resid[:, pl.ds(pl.multiple_of(head * WIDTH, WIDTH), WIDTH)]
    f_recv()
    total = own + ((fin_all[0].astype(F32) + fin_all[1].astype(F32))
                   + (fin_all[2].astype(F32) + fin_all[3].astype(F32)))
    for group in far_returns:
        group[0]()
    mixed = dot(mix[:, :FIRST * ROWS], far_ret[...].reshape(FIRST * ROWS, 256))
    total = total + jnp.concatenate([mixed[0:16] + mixed[16:32], mixed[32:48] + mixed[48:64]], axis=1)
    out_ref[...] = total.astype(BF16)
    f_sent()
    for group in far_returns:
        group[1]()


def body(hidden_in, gain_attn, gain_moe, w_query, w_key, w_value, w_out, w_router, w_gate, w_up, w_down,
         cache_kv, parked_kv, lengths, cache_source, expert_ids):
    half = HD // 2
    freq = 50000.0 ** (-2.0 * np.arange(half, dtype=np.float64) / HD)
    table = np.zeros((8, NREQ * ROWS), np.float32)
    table[0, :HD] = np.concatenate([freq, freq])
    table[1:4] = np.repeat(np.asarray(OFFSETS).T, ROWS, axis=1)
    table[4:7, :3 * NREQ] = np.tile(np.asarray(OFFSETS).T, (1, 3))
    hbm = pl.BlockSpec(memory_space=pl.ANY)
    dma = pltpu.SemaphoreType.DMA
    operands = [hidden_in, gain_attn.reshape(1, D), gain_moe.reshape(1, D), jnp.asarray(table),
                lengths.reshape(1, -1), cache_source.reshape(1, -1), expert_ids.T,
                w_query, w_key, w_value, w_out, w_router.T, w_gate, w_up, w_down, cache_kv, parked_kv]
    q_block = (NREQ, ROWS, 256)
    wide = (NREQ, ROWS, 1024)
    return pl.pallas_call(
        kernel,
        out_shape=jax.ShapeDtypeStruct((ROWS, WIDTH), BF16),
        in_specs=[hbm] * len(operands),
        out_specs=pl.BlockSpec(memory_space=pltpu.VMEM),
        scratch_shapes=[pltpu.VMEM(x.shape, x.dtype) for x in operands] + [
            pltpu.VMEM(q_block[1:], BF16), pltpu.VMEM(q_block, BF16),
            pltpu.VMEM(q_block[1:], BF16), pltpu.VMEM(q_block, BF16),
            pltpu.VMEM((1, HD), F32), pltpu.VMEM((NREQ, 1, HD), F32),
            pltpu.VMEM((NHEAD, ROWS, 1024), BF16), pltpu.VMEM((NHEAD, ROWS, 1024), BF16),
            pltpu.VMEM(wide, BF16), pltpu.VMEM(wide, BF16),
            pltpu.VMEM(wide, BF16), pltpu.VMEM(wide, BF16),
            pltpu.VMEM((NHEAD, FIRST, ROWS, 256), BF16),
            pltpu.VMEM((FIRST, ROWS, 256), BF16), pltpu.VMEM((FIRST, ROWS, 256), BF16),
            pltpu.VMEM((NHEAD, ROWS, WIDTH), BF16), pltpu.VMEM((NHEAD, ROWS, WIDTH), BF16),
            pltpu.VMEM((ROWS, D), F32),
            dma((len(operands),)),
            dma((1,)), dma((1,)), dma((2,)), dma((2,)),
            dma((2, NHEAD)), dma((2, NHEAD)),
            dma((4,)), dma((4,)), dma((2, NHEAD)), dma((2, NHEAD)), dma((2, NHEAD)), dma((2, NHEAD)),
            dma((2,)), dma((2,)), dma((2,)), dma((2,)),
            dma((NHEAD,)), dma((NHEAD,)),
        ],
        compiler_params=pltpu.CompilerParams(
            collective_id=0, has_side_effects=True, vmem_limit_bytes=60 * 1024 * 1024),
    )(*operands)


def solution(mesh):
    placed = (
        P("req", None),
        P(),
        P(),
        P(None, "head"),
        P(None, "head"),
        P(None, "head"),
        P("head", None),
        P(),
        P("req", None, "head"),
        P("req", None, "head"),
        P("req", "head", None),
        P(None, "req", None, "head"),
        P(None, "req", None, "head"),
        P(),
        P(),
        P("req", None),
    )
    return jax.shard_map(
        body, mesh=mesh, in_specs=placed, out_specs=P("req", "head"), check_vma=False
    )
```

```python
import jax
import jax.numpy as jnp
import numpy as np
from jax import lax
from jax.experimental import pallas as pl
from jax.experimental.pallas import tpu as pltpu
from jax.sharding import PartitionSpec as P

MESH = pl.DeviceIdType.MESH
F32 = jnp.float32
BF16 = jnp.bfloat16
I32 = jnp.int32

D = 2048
HD = 128
E = 64
NREQ = 32
NHEAD = 4
ROWS = 16
RES = 8
SPAN = 256
WIDTH = 512
FFL = 256
SCALE = HD ** (-0.5)


def ring(step):
    return min(step, 4 - step)


OFFSETS = sorted(
    ((dx, dz, dc) for dx in range(4) for dz in range(4) for dc in range(2)),
    key=lambda o: (-(ring(o[0]) + ring(o[1])), -o[2], abs(o[0] - o[1]), o))
FAR = ((0, 6), (6, 10))
NEAR = ((10, 22), (22, 32))
FIRST = 10
EPS = 1e-06


def iota(shape, dim):
    return lax.broadcasted_iota(I32, shape, dim)


def rms_scale(x, gain):
    inverse = lax.rsqrt(jnp.mean(x * x, axis=-1, keepdims=True) + EPS)
    return x * inverse * gain


def round_trip(x):
    return x.astype(BF16).astype(F32)


def dot(a, b):
    return jnp.dot(a, b, preferred_element_type=F32)


def split(x):
    blocks = [x[:, n * 256:(n + 1) * 256] for n in range(8)]
    return jnp.concatenate(blocks[::2], axis=1), jnp.concatenate(blocks[1::2], axis=1)


def join(even, odd):
    width = even.shape[1] // 256
    return jnp.concatenate(
        [part[:, n * 256:(n + 1) * 256] for n in range(width) for part in (even, odd)], axis=1)


def rotate(x, cosine, sine):
    parts = []
    for h in range(NHEAD):
        u = x[:, h * HD:(h + 1) * HD]
        parts.append(u * cosine + pltpu.roll(u, HD // 2, 1) * sine)
    return jnp.concatenate(parts, axis=1)


def cache_attention(q, row_lengths, kv, early=None):
    stacked = jnp.concatenate([q] * NHEAD, axis=0)
    row = iota((NHEAD * RES, WIDTH), 0)
    col = iota((NHEAD * RES, WIDTH), 1)
    stacked = jnp.where(row // RES == col // HD, stacked, 0.0)
    scores = jnp.zeros((NHEAD * RES, SPAN), F32)
    for i in range(RES):
        part = jnp.where(row % RES == i, stacked, 0.0).astype(BF16)
        scores = scores + lax.dot_general(
            part, kv[0, i], (((1,), (1,)), ((), ())), preferred_element_type=F32)
    scores = scores * SCALE
    limit = jnp.concatenate([row_lengths] * NHEAD, axis=0)
    usable = iota((NHEAD * RES, SPAN), 1).astype(F32) < limit
    scores = jnp.where(usable, scores, -1e30)
    row_max = jnp.max(scores, axis=1, keepdims=True)
    weights = jnp.where(usable, jnp.exp(scores - row_max), 0.0)
    row_total = jnp.sum(weights, axis=1, keepdims=True)
    if early is not None:
        early(row_max, row_total)
    probs = weights.astype(BF16)
    pieces = [jnp.zeros((RES, HD), F32)] * NHEAD
    small = iota((RES, HD), 0)
    for i in range(RES):
        out = dot(probs, kv[1, i])
        for h in range(NHEAD):
            pieces[h] = jnp.where(
                small == i, out[h * RES:(h + 1) * RES, h * HD:(h + 1) * HD], pieces[h])
    maxes = [row_max[h * RES:(h + 1) * RES] for h in range(NHEAD)]
    totals = [row_total[h * RES:(h + 1) * RES] for h in range(NHEAD)]
    normal = [pieces[h] / totals[h] for h in range(NHEAD)]
    return normal, maxes, totals


def kernel(
    hidden_hbm, gain_a_hbm, gain_m_hbm, table_hbm, lengths_hbm, source_hbm, ids_hbm,
    wq_hbm, wk_hbm, wv_hbm, wo_hbm, wr_hbm, wg_hbm, wu_hbm, wd_hbm, cache_hbm, parked_hbm,
    out_ref,
    hidden_ref, gain_a_ref, gain_m_ref, table_ref, lengths_ref, source_ref, ids_ref,
    wq, wk, wv, wo, wr, wg, wu, wd, cache, parked,
    q_send, q_all, a_send, a_all, st_send, st_all, home_all, back_all, disp, arrived, ret_send, ret,
    part_all, far_send, far_ret, fin_send, fin_all, resid,
    load_sem, q_ss, q_rs, a_ss, a_rs, h_ss, h_rs, d_ss, d_rs, y_ss, y_rs, p_ss, p_rs, t_ss, t_rs,
    r_ss, r_rs, f_ss, f_rs,
):
    me = lax.axis_index("req")
    head = lax.axis_index("head")
    my_x, my_z, my_c = me // 8, (me // 2) % 4, me % 2

    def ahead(n):
        dx, dz, dc = OFFSETS[n]
        return ((my_x + dx) % 4) * 8 + ((my_z + dz) % 4) * 2 + (my_c + dc) % 2

    def behind(n):
        dx, dz, dc = OFFSETS[n]
        return ((my_x + 4 - dx) % 4) * 8 + ((my_z + 4 - dz) % 4) * 2 + (my_c + dc) % 2

    barrier = pltpu.get_barrier_semaphore()
    for n in range(NREQ - 1):
        pl.semaphore_signal(barrier, inc=1, device_id={"req": ahead(n)}, device_id_type=MESH)
    for d in range(1, NHEAD):
        pl.semaphore_signal(barrier, inc=1, device_id={"head": (head + d) % NHEAD}, device_id_type=MESH)

    loads = {}
    order = [("hidden", hidden_hbm, hidden_ref), ("gain_a", gain_a_hbm, gain_a_ref),
             ("table", table_hbm, table_ref), ("lengths", lengths_hbm, lengths_ref),
             ("wq", wq_hbm, wq), ("source", source_hbm, source_ref), ("ids", ids_hbm, ids_ref),
             ("gain_m", gain_m_hbm, gain_m_ref),
             ("wk", wk_hbm, wk), ("wv", wv_hbm, wv), ("cache", cache_hbm, cache),
             ("parked", parked_hbm, parked), ("wo", wo_hbm, wo), ("wr", wr_hbm, wr),
             ("wg", wg_hbm, wg), ("wu", wu_hbm, wu), ("wd", wd_hbm, wd)]
    for n, (name, src, dst) in enumerate(order):
        loads[name] = pltpu.make_async_copy(src, dst, load_sem.at[n])
        loads[name].start()

    def launch(lo, hi, source, landing, ss, rs, target):
        hi = min(hi, NREQ - 1)
        for n in range(lo, hi):
            pltpu.make_async_remote_copy(
                src_ref=source(n), dst_ref=landing(n), send_sem=ss, recv_sem=rs,
                device_id={"req": target(n)}, device_id_type=MESH).start()
        span = landing(pl.ds(lo, hi - lo))
        whole = pltpu.make_async_remote_copy(
            src_ref=span, dst_ref=span, send_sem=ss, recv_sem=rs,
            device_id={"req": target(lo)}, device_id_type=MESH)
        return whole.wait_recv, whole.wait_send

    def head_exchange(source, landing, ss, rs):
        def copy(d, own):
            peer = (head + d) % NHEAD
            return pltpu.make_async_remote_copy(
                src_ref=source(peer), dst_ref=landing(head if own else peer), send_sem=ss.at[d],
                recv_sem=rs.at[head if own else peer], device_id={"head": peer}, device_id_type=MESH)

        mine = [copy(d, True) for d in range(1, NHEAD)]
        theirs = [copy(d, False) for d in range(1, NHEAD)]
        for move in mine:
            move.start()
        return (lambda: [move.wait_recv() for move in theirs]), (lambda: [move.wait_send() for move in mine])

    for name in ("hidden", "gain_a", "table", "lengths"):
        loads[name].wait()
    hidden = hidden_ref[...].astype(F32)
    normed = rms_scale(hidden, gain_a_ref[...]).astype(BF16)
    pick = iota((ROWS, NREQ * ROWS), 1) == me * ROWS + iota((ROWS, NREQ * ROWS), 0)
    lengths = lengths_ref[...].astype(F32)
    own_len = jnp.sum(jnp.where(pick, lengths, 0.0), axis=1, keepdims=True)
    angles = own_len * table_ref[0:1, :HD]
    cosine = jnp.cos(angles)
    sine = jnp.sin(angles)
    sine = jnp.where(iota((ROWS, HD), 1) < HD // 2, -sine, sine)
    loads["wq"].wait()
    q = round_trip(rotate(dot(normed, wq[...]), cosine, sine))
    q_block = jnp.concatenate([q[RES:, :256], q[RES:, 256:]], axis=0).astype(BF16)
    q_send[...] = q_block
    q_all[NREQ - 1] = q_block

    wide = NREQ * ROWS
    g_row = iota((ROWS, wide), 0)
    g_col = iota((ROWS, wide), 1)
    same_half = g_row // RES == (g_col % ROWS) // RES
    step_x = table_ref[1:2, :].astype(I32)
    step_z = table_ref[2:3, :].astype(I32)
    step_c = table_ref[3:4, :].astype(I32)
    src = ((my_x + 4 - step_x) % 4) * 8 + ((my_z + 4 - step_z) % 4) * 2 + (my_c + step_c) % 2
    dst = ((my_x + step_x) % 4) * 8 + ((my_z + step_z) % 4) * 2 + (my_c + step_c) % 2
    place = src * RES + iota((1, wide), 1) % RES
    natural = iota((256, wide), 1)
    spread = jnp.concatenate([
        (iota((256, wide), 0) == place).astype(F32),
        ((iota((256, wide), 0) == (natural // ROWS) * RES + natural % RES)
         & (natural % ROWS >= RES)).astype(F32)], axis=1).astype(BF16)
    loads["source"].wait()
    source = source_ref[...].astype(F32)
    source_wide = dot(jnp.broadcast_to(source, (RES, 256)).astype(BF16), spread)[0:1]
    hot_park = (same_half & (source_wide[:, :wide] == (me * RES + g_row % RES).astype(F32))).astype(F32).astype(BF16)
    row8 = iota((RES, wide), 0)
    hot_len = (source_wide[:, wide:] == (me * RES + row8).astype(F32)) & (iota((RES, wide), 1) % ROWS >= RES)
    park_len = jnp.sum(jnp.where(hot_len, lengths, 0.0), axis=1, keepdims=True)
    pick = iota((ROWS, 256), 1) == me * RES + iota((ROWS, 256), 0) % RES
    own_source = jnp.sum(jnp.where(pick, source, 0.0), axis=1, keepdims=True)
    block_src = table_ref[4:7, :3 * NREQ].astype(I32)
    block_src = (((my_x + 4 - block_src[0:1]) % 4) * 8 + ((my_z + 4 - block_src[1:2]) % 4) * 2
                 + (my_c + block_src[2:3]) % 2)
    hot_block = (jnp.floor(own_source[:RES] / RES) == block_src.astype(F32)).astype(F32).astype(BF16)
    hot_home = (same_half & (own_source == place.astype(F32))).astype(F32).astype(BF16)

    pl.semaphore_wait(barrier, NREQ - 1 + NHEAD - 1)
    q_recv, q_sent = launch(0, NREQ, lambda n: q_send, lambda n: q_all.at[n], q_ss.at[0], q_rs.at[0], ahead)

    loads["wk"].wait()
    k = round_trip(rotate(dot(normed, wk[...]), cosine, sine))
    loads["wv"].wait()
    v = round_trip(dot(normed, wv[...]))
    loads["cache"].wait()
    home_a, home_m, home_t = cache_attention(q[:RES], own_len[:RES], cache)
    new_score = [SCALE * jnp.sum(q[:, h * HD:(h + 1) * HD] * k[:, h * HD:(h + 1) * HD], axis=1, keepdims=True)
                 for h in range(NHEAD)]

    def merge_weights(first, m, t):
        pairs = []
        for h in range(NHEAD):
            score = new_score[h][first:first + RES]
            top = jnp.maximum(m[h], score)
            old = t[h] * jnp.exp(m[h] - top)
            new = jnp.exp(score - top)
            total = old + new
            pairs.append((jnp.broadcast_to(old / total, (RES, HD)),
                          v[first:first + RES, h * HD:(h + 1) * HD] * (new / total)))
        return pairs

    def finish(pairs, a):
        pieces = [a[h] * pairs[h][0] + pairs[h][1] for h in range(NHEAD)]
        out = dot(jnp.concatenate(pieces, axis=1).astype(BF16), wo[...])
        return jnp.concatenate([out[:, :1024], out[:, 1024:]], axis=0).astype(BF16)

    def summed(parts):
        whole = (parts[0].astype(F32) + parts[1].astype(F32)) + (parts[2].astype(F32) + parts[3].astype(F32))
        return jnp.concatenate([whole[:RES], whole[RES:]], axis=1)

    loads["wo"].wait()
    home_all[head] = finish(merge_weights(0, home_m, home_t), home_a)
    home_recv, home_sent = head_exchange(lambda p: home_all.at[head], lambda p: home_all.at[p], h_ss.at[0], h_rs.at[0])
    loads["parked"].wait()

    q_recv()
    parked_q = dot(hot_park, q_all[...].reshape(wide, 256))
    stat_moves = []

    def send_stats(row_max, row_total):
        stats = jnp.concatenate([row_max, row_total], axis=0)
        shape = (2 * NHEAD * RES, HD)
        stats = jnp.sum(jnp.where(iota(shape, 0) == iota(shape, 1), stats, 0.0), axis=0, keepdims=True)
        st_send[...] = stats
        st_all[NREQ - 1] = stats
        stat_moves.extend(launch(
            0, NREQ, lambda n: st_send, lambda n: st_all.at[n], a_ss.at[1], a_rs.at[1], ahead))

    park_a, park_m, park_t = cache_attention(
        jnp.concatenate([parked_q[:RES], parked_q[RES:]], axis=1), park_len, parked, send_stats)
    st_recv, st_sent = stat_moves

    a_block = jnp.concatenate([
        jnp.concatenate(park_a[:2], axis=1), jnp.concatenate(park_a[2:], axis=1)], axis=0).astype(BF16)
    a_send[...] = a_block
    a_recv, a_sent = launch(0, NREQ, lambda n: a_send, lambda n: a_all.at[n], a_ss.at[0], a_rs.at[0], ahead)
    a_all[NREQ - 1] = a_block
    q_sent()

    loads["ids"].wait()
    ids = ids_ref[...]
    expert = iota((E, ROWS), 0)
    chosen_t = jnp.zeros((E, ROWS), F32)
    for n in range(ids.shape[0]):
        chosen_t = jnp.where(ids[n:n + 1] == expert, 1.0, chosen_t)
    before = iota((ROWS, ROWS), 1) < iota((ROWS, ROWS), 0)
    same = iota((ROWS, ROWS), 1) == iota((ROWS, ROWS), 0)
    both = jnp.concatenate([same.astype(F32), before.astype(F32)], axis=0).astype(BF16)
    chosen_rank = lax.dot_general(
        both, chosen_t.astype(BF16), (((1,), (1,)), ((), ())), preferred_element_type=F32)
    chosen = chosen_rank[:ROWS]
    expand = (iota((E, wide), 0) == dst * 2 + (iota((1, wide), 1) % RES) // 4).astype(F32).astype(BF16)
    placed = dot(chosen_rank.astype(BF16), expand)
    taken = jnp.where((placed[:ROWS] > 0.5) & (placed[ROWS:] == (g_col % 4).astype(F32)), 1.0, 0.0)
    low_half = (g_col % ROWS) // RES == 0
    taken_halves = jnp.concatenate([jnp.where(low_half, taken, 0.0), jnp.where(low_half, 0.0, taken)], axis=0)
    taken_t = taken_halves.T.astype(BF16)
    loads["gain_m"].wait()
    home_recv()
    home_residual = hidden[:RES] + summed(home_all)

    st_recv()
    st = st_all[...].reshape(NREQ, HD)
    st0 = round_trip(st)
    st1 = round_trip(st - st0)
    st = jnp.concatenate([st0, st1, st - st0 - st1], axis=0).astype(BF16)
    picked = dot(hot_block, st)
    lane = iota((RES, HD), 1).astype(F32)
    turn = own_source[:RES] - jnp.floor(own_source[:RES] / RES) * RES
    back_s = [jnp.sum(jnp.where(lane == turn + n * RES, picked, 0.0), axis=1, keepdims=True)
              for n in range(2 * NHEAD)]
    back_pairs = merge_weights(RES, back_s[:NHEAD], back_s[NHEAD:])

    a_recv()
    back = dot(hot_home, a_all[...].reshape(wide, 256))
    back_a = [back[(h // 2) * RES:(h // 2 + 1) * RES, (h % 2) * HD:(h % 2 + 1) * HD] for h in range(NHEAD)]
    back_all[head] = finish(back_pairs, back_a)
    h_recv, h_sent = head_exchange(lambda p: back_all.at[head], lambda p: back_all.at[p], h_ss.at[1], h_rs.at[1])
    a_sent()
    st_sent()
    home_sent()
    loads["wr"].wait()
    h_recv()
    residual = jnp.concatenate([home_residual, hidden[RES:] + summed(back_all)], axis=0)
    normed_f = round_trip(rms_scale(residual, gain_m_ref[...]))

    stacked = jnp.concatenate(split(normed_f), axis=0).astype(BF16)
    disp[...] = dot(taken_t, stacked).astype(BF16).reshape(NREQ, ROWS, 1024)
    def quarter(p):
        return pl.ds(pl.multiple_of(p * 256, 256), 256)

    far_moves = [launch(lo, hi, lambda n: disp.at[n, :, quarter(head)], lambda n: arrived.at[n, :, quarter(head)],
                        d_ss.at[g], d_rs.at[g], ahead) for g, (lo, hi) in enumerate(FAR)]
    moves = [launch(lo, hi, lambda n: disp.at[n], lambda n: arrived.at[n], d_ss.at[2 + g], d_rs.at[2 + g], ahead)
             for g, (lo, hi) in enumerate(NEAR)]
    arrived[NREQ - 1] = disp[NREQ - 1]
    resid[...] = residual
    h_sent()

    logits = lax.dot_general(
        normed_f.astype(BF16), wr[...], (((1,), (1,)), ((), ())), preferred_element_type=F32)
    hit = chosen > 0.5
    top = jnp.max(jnp.where(hit, logits, -3e38), axis=1, keepdims=True)
    power = jnp.where(hit, jnp.exp(jnp.where(hit, logits, top) - top), 0.0)
    gates = power / jnp.sum(power, axis=1, keepdims=True)
    g_hi = round_trip(gates)
    gate_wide = dot(jnp.concatenate([g_hi, gates - g_hi], axis=0).astype(BF16), expand)
    mix_hi = gate_wide[:ROWS] * taken
    mix_lo = gate_wide[ROWS:] * taken
    mix = jnp.concatenate([
        jnp.where(low_half, mix_hi, 0.0), jnp.where(low_half, mix_lo, 0.0),
        jnp.where(low_half, 0.0, mix_hi), jnp.where(low_half, 0.0, mix_lo)], axis=0).astype(BF16)

    loads["wg"].wait()
    loads["wu"].wait()
    loads["wd"].wait()
    def experts(lo, hi):
        count = hi - lo
        tokens = arrived[lo:hi].astype(F32).reshape(count, 2, RES, 1024)
        tokens = join(tokens[:, 0].reshape(count * RES, 1024), tokens[:, 1].reshape(count * RES, 1024)).astype(BF16)
        which = (iota((count * RES, FFL), 0) % RES) // 4
        inner = []
        for e in range(2):
            gate = dot(tokens, wg[e])
            up = dot(tokens, wu[e])
            act = gate / (1.0 + jnp.exp(-gate)) * up
            inner.append(jnp.where(which == e, act, 0.0).astype(BF16))
        out = dot(inner[0], wd[0]) + dot(inner[1], wd[1])
        out = [part.reshape(count, RES, 1024) for part in split(out)]
        ret_send[lo:hi] = jnp.concatenate(out, axis=1).astype(BF16)

    def give_back(g):
        lo, hi = NEAR[g]
        return launch(lo, hi, lambda n: ret_send.at[n], lambda n: ret.at[n], r_ss.at[g], r_rs.at[g], behind)

    swaps = []
    for g, (lo, hi) in enumerate(FAR):
        far_moves[g][0]()
        swaps.append(head_exchange(
            lambda p: arrived.at[pl.ds(lo, hi - lo), :, quarter(head)],
            lambda p: arrived.at[pl.ds(lo, hi - lo), :, quarter(p)], y_ss.at[g], y_rs.at[g]))
    returns = []
    for g, (lo, hi) in enumerate(NEAR):
        moves[g][0]()
        experts(lo, hi)
        returns.append(give_back(g))
    ret[NREQ - 1] = ret_send[NREQ - 1]
    parts = []
    for g, (lo, hi) in enumerate(FAR):
        swaps[g][0]()
        experts(lo, hi)
        parts.append(head_exchange(
            lambda p: ret_send.at[pl.ds(lo, hi - lo), :, quarter(p)],
            lambda p: part_all.at[p, pl.ds(lo, hi - lo)], p_ss.at[g], p_rs.at[g]))
        part_all[head, lo:hi] = ret_send[lo:hi, :, quarter(head)]
    far_returns = []
    for g, (lo, hi) in enumerate(FAR):
        parts[g][0]()
        whole = [part_all[h, lo:hi].astype(F32) for h in range(NHEAD)]
        far_send[lo:hi] = ((whole[0] + whole[1]) + (whole[2] + whole[3])).astype(BF16)
        far_returns.append(launch(
            lo, hi, lambda n: far_send.at[n], lambda n: far_ret.at[n], t_ss.at[g], t_rs.at[g], behind))
    for back_move in returns:
        back_move[0]()
    mixed = dot(mix[:, FIRST * ROWS:], ret[FIRST:].reshape(wide - FIRST * ROWS, 1024))
    mixture = join(mixed[0:16] + mixed[16:32], mixed[32:48] + mixed[48:64])
    for h in range(NHEAD):
        fin_send[h] = mixture[:, h * WIDTH:(h + 1) * WIDTH].astype(BF16)
    f_recv, f_sent = head_exchange(lambda p: fin_send.at[p], lambda p: fin_all.at[p], f_ss, f_rs)
    fin_all[head] = fin_send[head]
    for group in swaps + parts + far_moves + moves + returns:
        group[1]()
    own = resid[:, pl.ds(pl.multiple_of(head * WIDTH, WIDTH), WIDTH)]
    f_recv()
    total = own + ((fin_all[0].astype(F32) + fin_all[1].astype(F32))
                   + (fin_all[2].astype(F32) + fin_all[3].astype(F32)))
    for group in far_returns:
        group[0]()
    mixed = dot(mix[:, :FIRST * ROWS], far_ret[...].reshape(FIRST * ROWS, 256))
    total = total + jnp.concatenate([mixed[0:16] + mixed[16:32], mixed[32:48] + mixed[48:64]], axis=1)
    out_ref[...] = total.astype(BF16)
    f_sent()
    for group in far_returns:
        group[1]()


def body(hidden_in, gain_attn, gain_moe, w_query, w_key, w_value, w_out, w_router, w_gate, w_up, w_down,
         cache_kv, parked_kv, lengths, cache_source, expert_ids):
    half = HD // 2
    freq = 50000.0 ** (-2.0 * np.arange(half, dtype=np.float64) / HD)
    table = np.zeros((8, NREQ * ROWS), np.float32)
    table[0, :HD] = np.concatenate([freq, freq])
    table[1:4] = np.repeat(np.asarray(OFFSETS).T, ROWS, axis=1)
    table[4:7, :3 * NREQ] = np.tile(np.asarray(OFFSETS).T, (1, 3))
    hbm = pl.BlockSpec(memory_space=pl.ANY)
    dma = pltpu.SemaphoreType.DMA
    operands = [hidden_in, gain_attn.reshape(1, D), gain_moe.reshape(1, D), jnp.asarray(table),
                lengths.reshape(1, -1), cache_source.reshape(1, -1), expert_ids.T,
                w_query, w_key, w_value, w_out, w_router.T, w_gate, w_up, w_down, cache_kv, parked_kv]
    q_block = (NREQ, ROWS, 256)
    wide = (NREQ, ROWS, 1024)
    return pl.pallas_call(
        kernel,
        out_shape=jax.ShapeDtypeStruct((ROWS, WIDTH), BF16),
        in_specs=[hbm] * len(operands),
        out_specs=pl.BlockSpec(memory_space=pltpu.VMEM),
        scratch_shapes=[pltpu.VMEM(x.shape, x.dtype) for x in operands] + [
            pltpu.VMEM(q_block[1:], BF16), pltpu.VMEM(q_block, BF16),
            pltpu.VMEM(q_block[1:], BF16), pltpu.VMEM(q_block, BF16),
            pltpu.VMEM((1, HD), F32), pltpu.VMEM((NREQ, 1, HD), F32),
            pltpu.VMEM((NHEAD, ROWS, 1024), BF16), pltpu.VMEM((NHEAD, ROWS, 1024), BF16),
            pltpu.VMEM(wide, BF16), pltpu.VMEM(wide, BF16),
            pltpu.VMEM(wide, BF16), pltpu.VMEM(wide, BF16),
            pltpu.VMEM((NHEAD, FIRST, ROWS, 256), BF16),
            pltpu.VMEM((FIRST, ROWS, 256), BF16), pltpu.VMEM((FIRST, ROWS, 256), BF16),
            pltpu.VMEM((NHEAD, ROWS, WIDTH), BF16), pltpu.VMEM((NHEAD, ROWS, WIDTH), BF16),
            pltpu.VMEM((ROWS, D), F32),
            dma((len(operands),)),
            dma((1,)), dma((1,)), dma((2,)), dma((2,)),
            dma((2, NHEAD)), dma((2, NHEAD)),
            dma((4,)), dma((4,)), dma((2, NHEAD)), dma((2, NHEAD)), dma((2, NHEAD)), dma((2, NHEAD)),
            dma((2,)), dma((2,)), dma((2,)), dma((2,)),
            dma((NHEAD,)), dma((NHEAD,)),
        ],
        compiler_params=pltpu.CompilerParams(
            collective_id=0, has_side_effects=True, vmem_limit_bytes=60 * 1024 * 1024),
    )(*operands)


def solution(mesh):
    placed = (
        P("req", None),
        P(),
        P(),
        P(None, "head"),
        P(None, "head"),
        P(None, "head"),
        P("head", None),
        P(),
        P("req", None, "head"),
        P("req", None, "head"),
        P("req", "head", None),
        P(None, "req", None, "head"),
        P(None, "req", None, "head"),
        P(),
        P(),
        P("req", None),
    )
    return jax.shard_map(
        body, mesh=mesh, in_specs=placed, out_specs=P("req", "head"), check_vma=False
    )
```

```python
import jax
import jax.numpy as jnp
import numpy as np
from jax import lax
from jax.experimental import pallas as pl
from jax.experimental.pallas import tpu as pltpu
from jax.sharding import PartitionSpec as P

MESH = pl.DeviceIdType.MESH
F32 = jnp.float32
BF16 = jnp.bfloat16
I32 = jnp.int32

D = 2048
HD = 128
E = 64
NREQ = 32
NHEAD = 4
ROWS = 16
RES = 8
SPAN = 256
WIDTH = 512
FFL = 256
SCALE = HD ** (-0.5)


def ring(step):
    return min(step, 4 - step)


OFFSETS = sorted(
    ((dx, dz, dc) for dx in range(4) for dz in range(4) for dc in range(2)),
    key=lambda o: (-(ring(o[0]) + ring(o[1])), -o[2], abs(o[0] - o[1]), o))
FAR = ((0, 4), (4, 10))
NEAR = ((10, 22), (22, 32))
FIRST = 10
EPS = 1e-06


def iota(shape, dim):
    return lax.broadcasted_iota(I32, shape, dim)


def rms_scale(x, gain):
    inverse = lax.rsqrt(jnp.mean(x * x, axis=-1, keepdims=True) + EPS)
    return x * inverse * gain


def round_trip(x):
    return x.astype(BF16).astype(F32)


def dot(a, b):
    return jnp.dot(a, b, preferred_element_type=F32)


def split(x):
    blocks = [x[:, n * 256:(n + 1) * 256] for n in range(8)]
    return jnp.concatenate(blocks[::2], axis=1), jnp.concatenate(blocks[1::2], axis=1)


def join(even, odd):
    width = even.shape[1] // 256
    return jnp.concatenate(
        [part[:, n * 256:(n + 1) * 256] for n in range(width) for part in (even, odd)], axis=1)


def rotate(x, cosine, sine):
    parts = []
    for h in range(NHEAD):
        u = x[:, h * HD:(h + 1) * HD]
        parts.append(u * cosine + pltpu.roll(u, HD // 2, 1) * sine)
    return jnp.concatenate(parts, axis=1)


def cache_attention(q, row_lengths, kv, early=None):
    stacked = jnp.concatenate([q] * NHEAD, axis=0)
    row = iota((NHEAD * RES, WIDTH), 0)
    col = iota((NHEAD * RES, WIDTH), 1)
    stacked = jnp.where(row // RES == col // HD, stacked, 0.0)
    scores = jnp.zeros((NHEAD * RES, SPAN), F32)
    for i in range(RES):
        part = jnp.where(row % RES == i, stacked, 0.0).astype(BF16)
        scores = scores + lax.dot_general(
            part, kv[0, i], (((1,), (1,)), ((), ())), preferred_element_type=F32)
    scores = scores * SCALE
    limit = jnp.concatenate([row_lengths] * NHEAD, axis=0)
    usable = iota((NHEAD * RES, SPAN), 1).astype(F32) < limit
    scores = jnp.where(usable, scores, -1e30)
    row_max = jnp.max(scores, axis=1, keepdims=True)
    weights = jnp.where(usable, jnp.exp(scores - row_max), 0.0)
    row_total = jnp.sum(weights, axis=1, keepdims=True)
    if early is not None:
        early(row_max, row_total)
    probs = weights.astype(BF16)
    pieces = [jnp.zeros((RES, HD), F32)] * NHEAD
    small = iota((RES, HD), 0)
    for i in range(RES):
        out = dot(probs, kv[1, i])
        for h in range(NHEAD):
            pieces[h] = jnp.where(
                small == i, out[h * RES:(h + 1) * RES, h * HD:(h + 1) * HD], pieces[h])
    maxes = [row_max[h * RES:(h + 1) * RES] for h in range(NHEAD)]
    totals = [row_total[h * RES:(h + 1) * RES] for h in range(NHEAD)]
    normal = [pieces[h] / totals[h] for h in range(NHEAD)]
    return normal, maxes, totals


def kernel(
    hidden_hbm, gain_a_hbm, gain_m_hbm, table_hbm, lengths_hbm, source_hbm, ids_hbm,
    wq_hbm, wk_hbm, wv_hbm, wo_hbm, wr_hbm, wg_hbm, wu_hbm, wd_hbm, cache_hbm, parked_hbm,
    out_ref,
    hidden_ref, gain_a_ref, gain_m_ref, table_ref, lengths_ref, source_ref, ids_ref,
    wq, wk, wv, wo, wr, wg, wu, wd, cache, parked,
    q_send, q_all, a_send, a_all, st_send, st_all, home_all, back_all, disp, arrived, ret_send, ret,
    part_all, far_send, far_ret, fin_send, fin_all, resid,
    load_sem, q_ss, q_rs, a_ss, a_rs, h_ss, h_rs, d_ss, d_rs, y_ss, y_rs, p_ss, p_rs, t_ss, t_rs,
    r_ss, r_rs, f_ss, f_rs,
):
    me = lax.axis_index("req")
    head = lax.axis_index("head")
    my_x, my_z, my_c = me // 8, (me // 2) % 4, me % 2

    def ahead(n):
        dx, dz, dc = OFFSETS[n]
        return ((my_x + dx) % 4) * 8 + ((my_z + dz) % 4) * 2 + (my_c + dc) % 2

    def behind(n):
        dx, dz, dc = OFFSETS[n]
        return ((my_x + 4 - dx) % 4) * 8 + ((my_z + 4 - dz) % 4) * 2 + (my_c + dc) % 2

    barrier = pltpu.get_barrier_semaphore()
    for n in range(NREQ - 1):
        pl.semaphore_signal(barrier, inc=1, device_id={"req": ahead(n)}, device_id_type=MESH)
    for d in range(1, NHEAD):
        pl.semaphore_signal(barrier, inc=1, device_id={"head": (head + d) % NHEAD}, device_id_type=MESH)

    loads = {}
    order = [("hidden", hidden_hbm, hidden_ref), ("gain_a", gain_a_hbm, gain_a_ref),
             ("table", table_hbm, table_ref), ("lengths", lengths_hbm, lengths_ref),
             ("wq", wq_hbm, wq), ("source", source_hbm, source_ref), ("ids", ids_hbm, ids_ref),
             ("gain_m", gain_m_hbm, gain_m_ref),
             ("wk", wk_hbm, wk), ("wv", wv_hbm, wv), ("cache", cache_hbm, cache),
             ("parked", parked_hbm, parked), ("wo", wo_hbm, wo), ("wr", wr_hbm, wr),
             ("wg", wg_hbm, wg), ("wu", wu_hbm, wu), ("wd", wd_hbm, wd)]
    for n, (name, src, dst) in enumerate(order):
        loads[name] = pltpu.make_async_copy(src, dst, load_sem.at[n])
        loads[name].start()

    def launch(lo, hi, source, landing, ss, rs, target):
        hi = min(hi, NREQ - 1)
        for n in range(lo, hi):
            pltpu.make_async_remote_copy(
                src_ref=source(n), dst_ref=landing(n), send_sem=ss, recv_sem=rs,
                device_id={"req": target(n)}, device_id_type=MESH).start()
        span = landing(pl.ds(lo, hi - lo))
        whole = pltpu.make_async_remote_copy(
            src_ref=span, dst_ref=span, send_sem=ss, recv_sem=rs,
            device_id={"req": target(lo)}, device_id_type=MESH)
        return whole.wait_recv, whole.wait_send

    def head_exchange(source, landing, ss, rs):
        def copy(d, own):
            peer = (head + d) % NHEAD
            return pltpu.make_async_remote_copy(
                src_ref=source(peer), dst_ref=landing(head if own else peer), send_sem=ss.at[d],
                recv_sem=rs.at[head if own else peer], device_id={"head": peer}, device_id_type=MESH)

        mine = [copy(d, True) for d in range(1, NHEAD)]
        theirs = [copy(d, False) for d in range(1, NHEAD)]
        for move in mine:
            move.start()
        return (lambda: [move.wait_recv() for move in theirs]), (lambda: [move.wait_send() for move in mine])

    for name in ("hidden", "gain_a", "table", "lengths"):
        loads[name].wait()
    hidden = hidden_ref[...].astype(F32)
    normed = rms_scale(hidden, gain_a_ref[...]).astype(BF16)
    pick = iota((ROWS, NREQ * ROWS), 1) == me * ROWS + iota((ROWS, NREQ * ROWS), 0)
    lengths = lengths_ref[...].astype(F32)
    own_len = jnp.sum(jnp.where(pick, lengths, 0.0), axis=1, keepdims=True)
    angles = own_len * table_ref[0:1, :HD]
    cosine = jnp.cos(angles)
    sine = jnp.sin(angles)
    sine = jnp.where(iota((ROWS, HD), 1) < HD // 2, -sine, sine)
    loads["wq"].wait()
    q = round_trip(rotate(dot(normed, wq[...]), cosine, sine))
    q_block = jnp.concatenate([q[RES:, :256], q[RES:, 256:]], axis=0).astype(BF16)
    q_send[...] = q_block
    q_all[NREQ - 1] = q_block

    wide = NREQ * ROWS
    g_row = iota((ROWS, wide), 0)
    g_col = iota((ROWS, wide), 1)
    same_half = g_row // RES == (g_col % ROWS) // RES
    step_x = table_ref[1:2, :].astype(I32)
    step_z = table_ref[2:3, :].astype(I32)
    step_c = table_ref[3:4, :].astype(I32)
    src = ((my_x + 4 - step_x) % 4) * 8 + ((my_z + 4 - step_z) % 4) * 2 + (my_c + step_c) % 2
    dst = ((my_x + step_x) % 4) * 8 + ((my_z + step_z) % 4) * 2 + (my_c + step_c) % 2
    place = src * RES + iota((1, wide), 1) % RES
    natural = iota((256, wide), 1)
    spread = jnp.concatenate([
        (iota((256, wide), 0) == place).astype(F32),
        ((iota((256, wide), 0) == (natural // ROWS) * RES + natural % RES)
         & (natural % ROWS >= RES)).astype(F32)], axis=1).astype(BF16)
    loads["source"].wait()
    source = source_ref[...].astype(F32)
    source_wide = dot(jnp.broadcast_to(source, (RES, 256)).astype(BF16), spread)[0:1]
    hot_park = (same_half & (source_wide[:, :wide] == (me * RES + g_row % RES).astype(F32))).astype(F32).astype(BF16)
    row8 = iota((RES, wide), 0)
    hot_len = (source_wide[:, wide:] == (me * RES + row8).astype(F32)) & (iota((RES, wide), 1) % ROWS >= RES)
    park_len = jnp.sum(jnp.where(hot_len, lengths, 0.0), axis=1, keepdims=True)
    pick = iota((ROWS, 256), 1) == me * RES + iota((ROWS, 256), 0) % RES
    own_source = jnp.sum(jnp.where(pick, source, 0.0), axis=1, keepdims=True)
    block_src = table_ref[4:7, :3 * NREQ].astype(I32)
    block_src = (((my_x + 4 - block_src[0:1]) % 4) * 8 + ((my_z + 4 - block_src[1:2]) % 4) * 2
                 + (my_c + block_src[2:3]) % 2)
    hot_block = (jnp.floor(own_source[:RES] / RES) == block_src.astype(F32)).astype(F32).astype(BF16)
    hot_home = (same_half & (own_source == place.astype(F32))).astype(F32).astype(BF16)

    pl.semaphore_wait(barrier, NREQ - 1 + NHEAD - 1)
    q_recv, q_sent = launch(0, NREQ, lambda n: q_send, lambda n: q_all.at[n], q_ss.at[0], q_rs.at[0], ahead)

    loads["wk"].wait()
    k = round_trip(rotate(dot(normed, wk[...]), cosine, sine))
    loads["wv"].wait()
    v = round_trip(dot(normed, wv[...]))
    loads["cache"].wait()
    home_a, home_m, home_t = cache_attention(q[:RES], own_len[:RES], cache)
    new_score = [SCALE * jnp.sum(q[:, h * HD:(h + 1) * HD] * k[:, h * HD:(h + 1) * HD], axis=1, keepdims=True)
                 for h in range(NHEAD)]

    def merge_weights(first, m, t):
        pairs = []
        for h in range(NHEAD):
            score = new_score[h][first:first + RES]
            top = jnp.maximum(m[h], score)
            old = t[h] * jnp.exp(m[h] - top)
            new = jnp.exp(score - top)
            total = old + new
            pairs.append((jnp.broadcast_to(old / total, (RES, HD)),
                          v[first:first + RES, h * HD:(h + 1) * HD] * (new / total)))
        return pairs

    def finish(pairs, a):
        pieces = [a[h] * pairs[h][0] + pairs[h][1] for h in range(NHEAD)]
        out = dot(jnp.concatenate(pieces, axis=1).astype(BF16), wo[...])
        return jnp.concatenate([out[:, :1024], out[:, 1024:]], axis=0).astype(BF16)

    def summed(parts):
        whole = (parts[0].astype(F32) + parts[1].astype(F32)) + (parts[2].astype(F32) + parts[3].astype(F32))
        return jnp.concatenate([whole[:RES], whole[RES:]], axis=1)

    loads["parked"].wait()

    q_recv()
    parked_q = dot(hot_park, q_all[...].reshape(wide, 256))
    stat_moves = []

    def send_stats(row_max, row_total):
        stats = jnp.concatenate([row_max, row_total], axis=0)
        shape = (2 * NHEAD * RES, HD)
        stats = jnp.sum(jnp.where(iota(shape, 0) == iota(shape, 1), stats, 0.0), axis=0, keepdims=True)
        st_send[...] = stats
        st_all[NREQ - 1] = stats
        stat_moves.extend(launch(
            0, NREQ, lambda n: st_send, lambda n: st_all.at[n], a_ss.at[1], a_rs.at[1], ahead))

    park_a, park_m, park_t = cache_attention(
        jnp.concatenate([parked_q[:RES], parked_q[RES:]], axis=1), park_len, parked, send_stats)
    st_recv, st_sent = stat_moves

    a_block = jnp.concatenate([
        jnp.concatenate(park_a[:2], axis=1), jnp.concatenate(park_a[2:], axis=1)], axis=0).astype(BF16)
    a_send[...] = a_block
    a_recv, a_sent = launch(0, NREQ, lambda n: a_send, lambda n: a_all.at[n], a_ss.at[0], a_rs.at[0], ahead)
    a_all[NREQ - 1] = a_block
    q_sent()

    loads["wo"].wait()
    home_all[head] = finish(merge_weights(0, home_m, home_t), home_a)
    home_recv, home_sent = head_exchange(lambda p: home_all.at[head], lambda p: home_all.at[p], h_ss.at[0], h_rs.at[0])

    loads["ids"].wait()
    ids = ids_ref[...]
    expert = iota((E, ROWS), 0)
    chosen_t = jnp.zeros((E, ROWS), F32)
    for n in range(ids.shape[0]):
        chosen_t = jnp.where(ids[n:n + 1] == expert, 1.0, chosen_t)
    before = iota((ROWS, ROWS), 1) < iota((ROWS, ROWS), 0)
    same = iota((ROWS, ROWS), 1) == iota((ROWS, ROWS), 0)
    both = jnp.concatenate([same.astype(F32), before.astype(F32)], axis=0).astype(BF16)
    chosen_rank = lax.dot_general(
        both, chosen_t.astype(BF16), (((1,), (1,)), ((), ())), preferred_element_type=F32)
    chosen = chosen_rank[:ROWS]
    expand = (iota((E, wide), 0) == dst * 2 + (iota((1, wide), 1) % RES) // 4).astype(F32).astype(BF16)
    placed = dot(chosen_rank.astype(BF16), expand)
    taken = jnp.where((placed[:ROWS] > 0.5) & (placed[ROWS:] == (g_col % 4).astype(F32)), 1.0, 0.0)
    low_half = (g_col % ROWS) // RES == 0
    taken_halves = jnp.concatenate([jnp.where(low_half, taken, 0.0), jnp.where(low_half, 0.0, taken)], axis=0)
    taken_t = taken_halves.T.astype(BF16)
    loads["gain_m"].wait()
    home_recv()
    home_residual = hidden[:RES] + summed(home_all)

    st_recv()
    st = st_all[...].reshape(NREQ, HD)
    st0 = round_trip(st)
    st1 = round_trip(st - st0)
    st = jnp.concatenate([st0, st1, st - st0 - st1], axis=0).astype(BF16)
    picked = dot(hot_block, st)
    lane = iota((RES, HD), 1).astype(F32)
    turn = own_source[:RES] - jnp.floor(own_source[:RES] / RES) * RES
    back_s = [jnp.sum(jnp.where(lane == turn + n * RES, picked, 0.0), axis=1, keepdims=True)
              for n in range(2 * NHEAD)]
    back_pairs = merge_weights(RES, back_s[:NHEAD], back_s[NHEAD:])

    a_recv()
    back = dot(hot_home, a_all[...].reshape(wide, 256))
    back_a = [back[(h // 2) * RES:(h // 2 + 1) * RES, (h % 2) * HD:(h % 2 + 1) * HD] for h in range(NHEAD)]
    back_all[head] = finish(back_pairs, back_a)
    h_recv, h_sent = head_exchange(lambda p: back_all.at[head], lambda p: back_all.at[p], h_ss.at[1], h_rs.at[1])
    a_sent()
    st_sent()
    home_sent()
    loads["wr"].wait()
    h_recv()
    residual = jnp.concatenate([home_residual, hidden[RES:] + summed(back_all)], axis=0)
    normed_f = round_trip(rms_scale(residual, gain_m_ref[...]))

    stacked = jnp.concatenate(split(normed_f), axis=0).astype(BF16)
    disp[:FIRST] = dot(taken_t[:FIRST * ROWS], stacked).astype(BF16).reshape(FIRST, ROWS, 1024)
    def quarter(p):
        return pl.ds(pl.multiple_of(p * 256, 256), 256)

    far_moves = [launch(lo, hi, lambda n: disp.at[n, :, quarter(head)], lambda n: arrived.at[n, :, quarter(head)],
                        d_ss.at[g], d_rs.at[g], ahead) for g, (lo, hi) in enumerate(FAR)]
    disp[FIRST:] = dot(taken_t[FIRST * ROWS:], stacked).astype(BF16).reshape(NREQ - FIRST, ROWS, 1024)
    moves = [launch(lo, hi, lambda n: disp.at[n], lambda n: arrived.at[n], d_ss.at[2 + g], d_rs.at[2 + g], ahead)
             for g, (lo, hi) in enumerate(NEAR)]
    arrived[NREQ - 1] = disp[NREQ - 1]
    resid[...] = residual
    h_sent()

    logits = lax.dot_general(
        normed_f.astype(BF16), wr[...], (((1,), (1,)), ((), ())), preferred_element_type=F32)
    hit = chosen > 0.5
    top = jnp.max(jnp.where(hit, logits, -3e38), axis=1, keepdims=True)
    power = jnp.where(hit, jnp.exp(jnp.where(hit, logits, top) - top), 0.0)
    gates = power / jnp.sum(power, axis=1, keepdims=True)
    g_hi = round_trip(gates)
    gate_wide = dot(jnp.concatenate([g_hi, gates - g_hi], axis=0).astype(BF16), expand)
    mix_hi = gate_wide[:ROWS] * taken
    mix_lo = gate_wide[ROWS:] * taken
    mix = jnp.concatenate([
        jnp.where(low_half, mix_hi, 0.0), jnp.where(low_half, mix_lo, 0.0),
        jnp.where(low_half, 0.0, mix_hi), jnp.where(low_half, 0.0, mix_lo)], axis=0).astype(BF16)

    loads["wg"].wait()
    loads["wu"].wait()
    loads["wd"].wait()
    def experts(lo, hi):
        count = hi - lo
        tokens = arrived[lo:hi].astype(F32).reshape(count, 2, RES, 1024)
        tokens = join(tokens[:, 0].reshape(count * RES, 1024), tokens[:, 1].reshape(count * RES, 1024)).astype(BF16)
        which = (iota((count * RES, FFL), 0) % RES) // 4
        inner = []
        for e in range(2):
            gate = dot(tokens, wg[e])
            up = dot(tokens, wu[e])
            act = gate / (1.0 + jnp.exp(-gate)) * up
            inner.append(jnp.where(which == e, act, 0.0).astype(BF16))
        out = dot(inner[0], wd[0]) + dot(inner[1], wd[1])
        out = [part.reshape(count, RES, 1024) for part in split(out)]
        ret_send[lo:hi] = jnp.concatenate(out, axis=1).astype(BF16)

    def give_back(g):
        lo, hi = NEAR[g]
        return launch(lo, hi, lambda n: ret_send.at[n], lambda n: ret.at[n], r_ss.at[g], r_rs.at[g], behind)

    swaps = []
    for g, (lo, hi) in enumerate(FAR):
        far_moves[g][0]()
        swaps.append(head_exchange(
            lambda p: arrived.at[pl.ds(lo, hi - lo), :, quarter(head)],
            lambda p: arrived.at[pl.ds(lo, hi - lo), :, quarter(p)], y_ss.at[g], y_rs.at[g]))
    returns = []

    def near(g):
        lo, hi = NEAR[g]
        moves[g][0]()
        experts(lo, hi)
        returns.append(give_back(g))

    near(0)
    parts = []
    for g, (lo, hi) in enumerate(FAR):
        swaps[g][0]()
        experts(lo, hi)
        parts.append(head_exchange(
            lambda p: ret_send.at[pl.ds(lo, hi - lo), :, quarter(p)],
            lambda p: part_all.at[p, pl.ds(lo, hi - lo)], p_ss.at[g], p_rs.at[g]))
        part_all[head, lo:hi] = ret_send[lo:hi, :, quarter(head)]
    near(1)
    ret[NREQ - 1] = ret_send[NREQ - 1]
    far_returns = []
    for g, (lo, hi) in enumerate(FAR):
        parts[g][0]()
        whole = [part_all[h, lo:hi].astype(F32) for h in range(NHEAD)]
        far_send[lo:hi] = ((whole[0] + whole[1]) + (whole[2] + whole[3])).astype(BF16)
        far_returns.append(launch(
            lo, hi, lambda n: far_send.at[n], lambda n: far_ret.at[n], t_ss.at[g], t_rs.at[g], behind))
    for back_move in returns:
        back_move[0]()
    mixed = dot(mix[:, FIRST * ROWS:], ret[FIRST:].reshape(wide - FIRST * ROWS, 1024))
    mixture = join(mixed[0:16] + mixed[16:32], mixed[32:48] + mixed[48:64])
    for h in range(NHEAD):
        fin_send[h] = mixture[:, h * WIDTH:(h + 1) * WIDTH].astype(BF16)
    f_recv, f_sent = head_exchange(lambda p: fin_send.at[p], lambda p: fin_all.at[p], f_ss, f_rs)
    fin_all[head] = fin_send[head]
    for group in swaps + parts + far_moves + moves + returns:
        group[1]()
    own = resid[:, pl.ds(pl.multiple_of(head * WIDTH, WIDTH), WIDTH)]
    f_recv()
    total = own + ((fin_all[0].astype(F32) + fin_all[1].astype(F32))
                   + (fin_all[2].astype(F32) + fin_all[3].astype(F32)))
    for group in far_returns:
        group[0]()
    mixed = dot(mix[:, :FIRST * ROWS], far_ret[...].reshape(FIRST * ROWS, 256))
    total = total + jnp.concatenate([mixed[0:16] + mixed[16:32], mixed[32:48] + mixed[48:64]], axis=1)
    out_ref[...] = total.astype(BF16)
    f_sent()
    for group in far_returns:
        group[1]()


def body(hidden_in, gain_attn, gain_moe, w_query, w_key, w_value, w_out, w_router, w_gate, w_up, w_down,
         cache_kv, parked_kv, lengths, cache_source, expert_ids):
    half = HD // 2
    freq = 50000.0 ** (-2.0 * np.arange(half, dtype=np.float64) / HD)
    table = np.zeros((8, NREQ * ROWS), np.float32)
    table[0, :HD] = np.concatenate([freq, freq])
    table[1:4] = np.repeat(np.asarray(OFFSETS).T, ROWS, axis=1)
    table[4:7, :3 * NREQ] = np.tile(np.asarray(OFFSETS).T, (1, 3))
    hbm = pl.BlockSpec(memory_space=pl.ANY)
    dma = pltpu.SemaphoreType.DMA
    operands = [hidden_in, gain_attn.reshape(1, D), gain_moe.reshape(1, D), jnp.asarray(table),
                lengths.reshape(1, -1), cache_source.reshape(1, -1), expert_ids.T,
                w_query, w_key, w_value, w_out, w_router.T, w_gate, w_up, w_down, cache_kv, parked_kv]
    q_block = (NREQ, ROWS, 256)
    wide = (NREQ, ROWS, 1024)
    return pl.pallas_call(
        kernel,
        out_shape=jax.ShapeDtypeStruct((ROWS, WIDTH), BF16),
        in_specs=[hbm] * len(operands),
        out_specs=pl.BlockSpec(memory_space=pltpu.VMEM),
        scratch_shapes=[pltpu.VMEM(x.shape, x.dtype) for x in operands] + [
            pltpu.VMEM(q_block[1:], BF16), pltpu.VMEM(q_block, BF16),
            pltpu.VMEM(q_block[1:], BF16), pltpu.VMEM(q_block, BF16),
            pltpu.VMEM((1, HD), F32), pltpu.VMEM((NREQ, 1, HD), F32),
            pltpu.VMEM((NHEAD, ROWS, 1024), BF16), pltpu.VMEM((NHEAD, ROWS, 1024), BF16),
            pltpu.VMEM(wide, BF16), pltpu.VMEM(wide, BF16),
            pltpu.VMEM(wide, BF16), pltpu.VMEM(wide, BF16),
            pltpu.VMEM((NHEAD, FIRST, ROWS, 256), BF16),
            pltpu.VMEM((FIRST, ROWS, 256), BF16), pltpu.VMEM((FIRST, ROWS, 256), BF16),
            pltpu.VMEM((NHEAD, ROWS, WIDTH), BF16), pltpu.VMEM((NHEAD, ROWS, WIDTH), BF16),
            pltpu.VMEM((ROWS, D), F32),
            dma((len(operands),)),
            dma((1,)), dma((1,)), dma((2,)), dma((2,)),
            dma((2, NHEAD)), dma((2, NHEAD)),
            dma((4,)), dma((4,)), dma((2, NHEAD)), dma((2, NHEAD)), dma((2, NHEAD)), dma((2, NHEAD)),
            dma((2,)), dma((2,)), dma((2,)), dma((2,)),
            dma((NHEAD,)), dma((NHEAD,)),
        ],
        compiler_params=pltpu.CompilerParams(
            collective_id=0, has_side_effects=True, vmem_limit_bytes=60 * 1024 * 1024),
    )(*operands)


def solution(mesh):
    placed = (
        P("req", None),
        P(),
        P(),
        P(None, "head"),
        P(None, "head"),
        P(None, "head"),
        P("head", None),
        P(),
        P("req", None, "head"),
        P("req", None, "head"),
        P("req", "head", None),
        P(None, "req", None, "head"),
        P(None, "req", None, "head"),
        P(),
        P(),
        P("req", None),
    )
    return jax.shard_map(
        body, mesh=mesh, in_specs=placed, out_specs=P("req", "head"), check_vma=False
    )
```

```python
import jax
import jax.numpy as jnp
import numpy as np
from jax import lax
from jax.experimental import pallas as pl
from jax.experimental.pallas import tpu as pltpu
from jax.sharding import PartitionSpec as P

MESH = pl.DeviceIdType.MESH
F32 = jnp.float32
BF16 = jnp.bfloat16
I32 = jnp.int32

D = 2048
HD = 128
E = 64
NREQ = 32
NHEAD = 4
ROWS = 16
RES = 8
SPAN = 256
WIDTH = 512
FFL = 256
SCALE = HD ** (-0.5)


def ring(step):
    return min(step, 4 - step)


OFFSETS = sorted(
    ((dx, dz, dc) for dx in range(4) for dz in range(4) for dc in range(2)),
    key=lambda o: (-(ring(o[0]) + ring(o[1])), -o[2], abs(o[0] - o[1]), o))
FAR = ((0, 4), (4, 10))
NEAR = ((10, 26), (26, 32))
FIRST = 10
EPS = 1e-06


def iota(shape, dim):
    return lax.broadcasted_iota(I32, shape, dim)


def rms_scale(x, gain):
    inverse = lax.rsqrt(jnp.mean(x * x, axis=-1, keepdims=True) + EPS)
    return x * inverse * gain


def round_trip(x):
    return x.astype(BF16).astype(F32)


def dot(a, b):
    return jnp.dot(a, b, preferred_element_type=F32)


def split(x):
    blocks = [x[:, n * 256:(n + 1) * 256] for n in range(8)]
    return jnp.concatenate(blocks[::2], axis=1), jnp.concatenate(blocks[1::2], axis=1)


def join(even, odd):
    width = even.shape[1] // 256
    return jnp.concatenate(
        [part[:, n * 256:(n + 1) * 256] for n in range(width) for part in (even, odd)], axis=1)


def rotate(x, cosine, sine):
    parts = []
    for h in range(NHEAD):
        u = x[:, h * HD:(h + 1) * HD]
        parts.append(u * cosine + pltpu.roll(u, HD // 2, 1) * sine)
    return jnp.concatenate(parts, axis=1)


def cache_attention(q, row_lengths, kv, early=None):
    stacked = jnp.concatenate([q] * NHEAD, axis=0)
    row = iota((NHEAD * RES, WIDTH), 0)
    col = iota((NHEAD * RES, WIDTH), 1)
    stacked = jnp.where(row // RES == col // HD, stacked, 0.0)
    scores = jnp.zeros((NHEAD * RES, SPAN), F32)
    for i in range(RES):
        part = jnp.where(row % RES == i, stacked, 0.0).astype(BF16)
        scores = scores + lax.dot_general(
            part, kv[0, i], (((1,), (1,)), ((), ())), preferred_element_type=F32)
    scores = scores * SCALE
    limit = jnp.concatenate([row_lengths] * NHEAD, axis=0)
    usable = iota((NHEAD * RES, SPAN), 1).astype(F32) < limit
    scores = jnp.where(usable, scores, -1e30)
    row_max = jnp.max(scores, axis=1, keepdims=True)
    weights = jnp.where(usable, jnp.exp(scores - row_max), 0.0)
    row_total = jnp.sum(weights, axis=1, keepdims=True)
    if early is not None:
        early(row_max, row_total)
    probs = weights.astype(BF16)
    pieces = [jnp.zeros((RES, HD), F32)] * NHEAD
    small = iota((RES, HD), 0)
    for i in range(RES):
        out = dot(probs, kv[1, i])
        for h in range(NHEAD):
            pieces[h] = jnp.where(
                small == i, out[h * RES:(h + 1) * RES, h * HD:(h + 1) * HD], pieces[h])
    maxes = [row_max[h * RES:(h + 1) * RES] for h in range(NHEAD)]
    totals = [row_total[h * RES:(h + 1) * RES] for h in range(NHEAD)]
    normal = [pieces[h] / totals[h] for h in range(NHEAD)]
    return normal, maxes, totals


def kernel(
    hidden_hbm, gain_a_hbm, gain_m_hbm, table_hbm, lengths_hbm, source_hbm, ids_hbm,
    wq_hbm, wk_hbm, wv_hbm, wo_hbm, wr_hbm, wg_hbm, wu_hbm, wd_hbm, cache_hbm, parked_hbm,
    out_ref,
    hidden_ref, gain_a_ref, gain_m_ref, table_ref, lengths_ref, source_ref, ids_ref,
    wq, wk, wv, wo, wr, wg, wu, wd, cache, parked,
    q_send, q_all, a_send, a_all, st_send, st_all, home_all, back_all, disp, arrived, ret_send, ret,
    part_all, far_send, far_ret, fin_send, fin_all, resid,
    load_sem, q_ss, q_rs, a_ss, a_rs, h_ss, h_rs, d_ss, d_rs, y_ss, y_rs, p_ss, p_rs, t_ss, t_rs,
    r_ss, r_rs, f_ss, f_rs,
):
    me = lax.axis_index("req")
    head = lax.axis_index("head")
    my_x, my_z, my_c = me // 8, (me // 2) % 4, me % 2

    def ahead(n):
        dx, dz, dc = OFFSETS[n]
        return ((my_x + dx) % 4) * 8 + ((my_z + dz) % 4) * 2 + (my_c + dc) % 2

    def behind(n):
        dx, dz, dc = OFFSETS[n]
        return ((my_x + 4 - dx) % 4) * 8 + ((my_z + 4 - dz) % 4) * 2 + (my_c + dc) % 2

    barrier = pltpu.get_barrier_semaphore()
    for n in range(NREQ - 1):
        pl.semaphore_signal(barrier, inc=1, device_id={"req": ahead(n)}, device_id_type=MESH)
    for d in range(1, NHEAD):
        pl.semaphore_signal(barrier, inc=1, device_id={"head": (head + d) % NHEAD}, device_id_type=MESH)

    loads = {}
    order = [("hidden", hidden_hbm, hidden_ref), ("gain_a", gain_a_hbm, gain_a_ref),
             ("table", table_hbm, table_ref), ("lengths", lengths_hbm, lengths_ref),
             ("wq", wq_hbm, wq), ("source", source_hbm, source_ref), ("ids", ids_hbm, ids_ref),
             ("gain_m", gain_m_hbm, gain_m_ref),
             ("wk", wk_hbm, wk), ("wv", wv_hbm, wv), ("cache", cache_hbm, cache),
             ("parked", parked_hbm, parked), ("wo", wo_hbm, wo), ("wr", wr_hbm, wr),
             ("wg", wg_hbm, wg), ("wu", wu_hbm, wu), ("wd", wd_hbm, wd)]
    for n, (name, src, dst) in enumerate(order):
        loads[name] = pltpu.make_async_copy(src, dst, load_sem.at[n])
        loads[name].start()

    def launch(lo, hi, source, landing, ss, rs, target):
        hi = min(hi, NREQ - 1)
        for n in range(lo, hi):
            pltpu.make_async_remote_copy(
                src_ref=source(n), dst_ref=landing(n), send_sem=ss, recv_sem=rs,
                device_id={"req": target(n)}, device_id_type=MESH).start()
        span = landing(pl.ds(lo, hi - lo))
        whole = pltpu.make_async_remote_copy(
            src_ref=span, dst_ref=span, send_sem=ss, recv_sem=rs,
            device_id={"req": target(lo)}, device_id_type=MESH)
        return whole.wait_recv, whole.wait_send

    def head_exchange(source, landing, ss, rs):
        def copy(d, own):
            peer = (head + d) % NHEAD
            return pltpu.make_async_remote_copy(
                src_ref=source(peer), dst_ref=landing(head if own else peer), send_sem=ss.at[d],
                recv_sem=rs.at[head if own else peer], device_id={"head": peer}, device_id_type=MESH)

        mine = [copy(d, True) for d in range(1, NHEAD)]
        theirs = [copy(d, False) for d in range(1, NHEAD)]
        for move in mine:
            move.start()
        return (lambda: [move.wait_recv() for move in theirs]), (lambda: [move.wait_send() for move in mine])

    for name in ("hidden", "gain_a", "table", "lengths"):
        loads[name].wait()
    hidden = hidden_ref[...].astype(F32)
    normed = rms_scale(hidden, gain_a_ref[...]).astype(BF16)
    pick = iota((ROWS, NREQ * ROWS), 1) == me * ROWS + iota((ROWS, NREQ * ROWS), 0)
    lengths = lengths_ref[...].astype(F32)
    own_len = jnp.sum(jnp.where(pick, lengths, 0.0), axis=1, keepdims=True)
    angles = own_len * table_ref[0:1, :HD]
    cosine = jnp.cos(angles)
    sine = jnp.sin(angles)
    sine = jnp.where(iota((ROWS, HD), 1) < HD // 2, -sine, sine)
    loads["wq"].wait()
    q = round_trip(rotate(dot(normed, wq[...]), cosine, sine))
    q_block = jnp.concatenate([q[RES:, :256], q[RES:, 256:]], axis=0).astype(BF16)
    q_send[...] = q_block
    q_all[NREQ - 1] = q_block

    wide = NREQ * ROWS
    g_row = iota((ROWS, wide), 0)
    g_col = iota((ROWS, wide), 1)
    same_half = g_row // RES == (g_col % ROWS) // RES
    step_x = table_ref[1:2, :].astype(I32)
    step_z = table_ref[2:3, :].astype(I32)
    step_c = table_ref[3:4, :].astype(I32)
    src = ((my_x + 4 - step_x) % 4) * 8 + ((my_z + 4 - step_z) % 4) * 2 + (my_c + step_c) % 2
    dst = ((my_x + step_x) % 4) * 8 + ((my_z + step_z) % 4) * 2 + (my_c + step_c) % 2
    place = src * RES + iota((1, wide), 1) % RES
    natural = iota((256, wide), 1)
    spread = jnp.concatenate([
        (iota((256, wide), 0) == place).astype(F32),
        ((iota((256, wide), 0) == (natural // ROWS) * RES + natural % RES)
         & (natural % ROWS >= RES)).astype(F32)], axis=1).astype(BF16)
    loads["source"].wait()
    source = source_ref[...].astype(F32)
    source_wide = dot(jnp.broadcast_to(source, (RES, 256)).astype(BF16), spread)[0:1]
    hot_park = (same_half & (source_wide[:, :wide] == (me * RES + g_row % RES).astype(F32))).astype(F32).astype(BF16)
    row8 = iota((RES, wide), 0)
    hot_len = (source_wide[:, wide:] == (me * RES + row8).astype(F32)) & (iota((RES, wide), 1) % ROWS >= RES)
    park_len = jnp.sum(jnp.where(hot_len, lengths, 0.0), axis=1, keepdims=True)
    pick = iota((ROWS, 256), 1) == me * RES + iota((ROWS, 256), 0) % RES
    own_source = jnp.sum(jnp.where(pick, source, 0.0), axis=1, keepdims=True)
    block_src = table_ref[4:7, :3 * NREQ].astype(I32)
    block_src = (((my_x + 4 - block_src[0:1]) % 4) * 8 + ((my_z + 4 - block_src[1:2]) % 4) * 2
                 + (my_c + block_src[2:3]) % 2)
    hot_block = (jnp.floor(own_source[:RES] / RES) == block_src.astype(F32)).astype(F32).astype(BF16)
    hot_home = (same_half & (own_source == place.astype(F32))).astype(F32).astype(BF16)

    pl.semaphore_wait(barrier, NREQ - 1 + NHEAD - 1)
    q_recv, q_sent = launch(0, NREQ, lambda n: q_send, lambda n: q_all.at[n], q_ss.at[0], q_rs.at[0], ahead)

    loads["wk"].wait()
    k = round_trip(rotate(dot(normed, wk[...]), cosine, sine))
    loads["wv"].wait()
    v = round_trip(dot(normed, wv[...]))
    loads["cache"].wait()
    home_a, home_m, home_t = cache_attention(q[:RES], own_len[:RES], cache)
    new_score = [SCALE * jnp.sum(q[:, h * HD:(h + 1) * HD] * k[:, h * HD:(h + 1) * HD], axis=1, keepdims=True)
                 for h in range(NHEAD)]

    def merge_weights(first, m, t):
        pairs = []
        for h in range(NHEAD):
            score = new_score[h][first:first + RES]
            top = jnp.maximum(m[h], score)
            old = t[h] * jnp.exp(m[h] - top)
            new = jnp.exp(score - top)
            total = old + new
            pairs.append((jnp.broadcast_to(old / total, (RES, HD)),
                          v[first:first + RES, h * HD:(h + 1) * HD] * (new / total)))
        return pairs

    def finish(pairs, a):
        pieces = [a[h] * pairs[h][0] + pairs[h][1] for h in range(NHEAD)]
        out = dot(jnp.concatenate(pieces, axis=1).astype(BF16), wo[...])
        return jnp.concatenate([out[:, :1024], out[:, 1024:]], axis=0).astype(BF16)

    def summed(parts):
        whole = (parts[0].astype(F32) + parts[1].astype(F32)) + (parts[2].astype(F32) + parts[3].astype(F32))
        return jnp.concatenate([whole[:RES], whole[RES:]], axis=1)

    loads["parked"].wait()

    q_recv()
    parked_q = dot(hot_park, q_all[...].reshape(wide, 256))
    stat_moves = []

    def send_stats(row_max, row_total):
        stats = jnp.concatenate([row_max, row_total], axis=0)
        shape = (2 * NHEAD * RES, HD)
        stats = jnp.sum(jnp.where(iota(shape, 0) == iota(shape, 1), stats, 0.0), axis=0, keepdims=True)
        st_send[...] = stats
        st_all[NREQ - 1] = stats
        stat_moves.extend(launch(
            0, NREQ, lambda n: st_send, lambda n: st_all.at[n], a_ss.at[1], a_rs.at[1], ahead))

    park_a, park_m, park_t = cache_attention(
        jnp.concatenate([parked_q[:RES], parked_q[RES:]], axis=1), park_len, parked, send_stats)
    st_recv, st_sent = stat_moves

    a_block = jnp.concatenate([
        jnp.concatenate(park_a[:2], axis=1), jnp.concatenate(park_a[2:], axis=1)], axis=0).astype(BF16)
    a_send[...] = a_block
    a_recv, a_sent = launch(0, NREQ, lambda n: a_send, lambda n: a_all.at[n], a_ss.at[0], a_rs.at[0], ahead)
    a_all[NREQ - 1] = a_block
    q_sent()

    loads["wo"].wait()
    home_all[head] = finish(merge_weights(0, home_m, home_t), home_a)
    home_recv, home_sent = head_exchange(lambda p: home_all.at[head], lambda p: home_all.at[p], h_ss.at[0], h_rs.at[0])

    loads["ids"].wait()
    ids = ids_ref[...]
    expert = iota((E, ROWS), 0)
    chosen_t = jnp.zeros((E, ROWS), F32)
    for n in range(ids.shape[0]):
        chosen_t = jnp.where(ids[n:n + 1] == expert, 1.0, chosen_t)
    before = iota((ROWS, ROWS), 1) < iota((ROWS, ROWS), 0)
    same = iota((ROWS, ROWS), 1) == iota((ROWS, ROWS), 0)
    both = jnp.concatenate([same.astype(F32), before.astype(F32)], axis=0).astype(BF16)
    chosen_rank = lax.dot_general(
        both, chosen_t.astype(BF16), (((1,), (1,)), ((), ())), preferred_element_type=F32)
    chosen = chosen_rank[:ROWS]
    expand = (iota((E, wide), 0) == dst * 2 + (iota((1, wide), 1) % RES) // 4).astype(F32).astype(BF16)
    placed = dot(chosen_rank.astype(BF16), expand)
    taken = jnp.where((placed[:ROWS] > 0.5) & (placed[ROWS:] == (g_col % 4).astype(F32)), 1.0, 0.0)
    low_half = (g_col % ROWS) // RES == 0
    taken_halves = jnp.concatenate([jnp.where(low_half, taken, 0.0), jnp.where(low_half, 0.0, taken)], axis=0)
    taken_t = taken_halves.T.astype(BF16)
    loads["gain_m"].wait()
    home_recv()
    home_residual = hidden[:RES] + summed(home_all)

    st_recv()
    st = st_all[...].reshape(NREQ, HD)
    st0 = round_trip(st)
    st1 = round_trip(st - st0)
    st = jnp.concatenate([st0, st1, st - st0 - st1], axis=0).astype(BF16)
    picked = dot(hot_block, st)
    lane = iota((RES, HD), 1).astype(F32)
    turn = own_source[:RES] - jnp.floor(own_source[:RES] / RES) * RES
    back_s = [jnp.sum(jnp.where(lane == turn + n * RES, picked, 0.0), axis=1, keepdims=True)
              for n in range(2 * NHEAD)]
    back_pairs = merge_weights(RES, back_s[:NHEAD], back_s[NHEAD:])

    a_recv()
    back = dot(hot_home, a_all[...].reshape(wide, 256))
    back_a = [back[(h // 2) * RES:(h // 2 + 1) * RES, (h % 2) * HD:(h % 2 + 1) * HD] for h in range(NHEAD)]
    back_all[head] = finish(back_pairs, back_a)
    h_recv, h_sent = head_exchange(lambda p: back_all.at[head], lambda p: back_all.at[p], h_ss.at[1], h_rs.at[1])
    a_sent()
    st_sent()
    home_sent()
    loads["wr"].wait()
    h_recv()
    residual = jnp.concatenate([home_residual, hidden[RES:] + summed(back_all)], axis=0)
    normed_f = round_trip(rms_scale(residual, gain_m_ref[...]))

    stacked = jnp.concatenate(split(normed_f), axis=0).astype(BF16)
    disp[:FIRST] = dot(taken_t[:FIRST * ROWS], stacked).astype(BF16).reshape(FIRST, ROWS, 1024)
    def quarter(p):
        return pl.ds(pl.multiple_of(p * 256, 256), 256)

    far_moves = [launch(lo, hi, lambda n: disp.at[n, :, quarter(head)], lambda n: arrived.at[n, :, quarter(head)],
                        d_ss.at[g], d_rs.at[g], ahead) for g, (lo, hi) in enumerate(FAR)]
    disp[FIRST:] = dot(taken_t[FIRST * ROWS:], stacked).astype(BF16).reshape(NREQ - FIRST, ROWS, 1024)
    moves = [launch(lo, hi, lambda n: disp.at[n], lambda n: arrived.at[n], d_ss.at[2 + g], d_rs.at[2 + g], ahead)
             for g, (lo, hi) in enumerate(NEAR)]
    arrived[NREQ - 1] = disp[NREQ - 1]
    resid[...] = residual
    h_sent()

    logits = lax.dot_general(
        normed_f.astype(BF16), wr[...], (((1,), (1,)), ((), ())), preferred_element_type=F32)
    hit = chosen > 0.5
    top = jnp.max(jnp.where(hit, logits, -3e38), axis=1, keepdims=True)
    power = jnp.where(hit, jnp.exp(jnp.where(hit, logits, top) - top), 0.0)
    gates = power / jnp.sum(power, axis=1, keepdims=True)
    g_hi = round_trip(gates)
    gate_wide = dot(jnp.concatenate([g_hi, gates - g_hi], axis=0).astype(BF16), expand)
    mix_hi = gate_wide[:ROWS] * taken
    mix_lo = gate_wide[ROWS:] * taken
    mix = jnp.concatenate([
        jnp.where(low_half, mix_hi, 0.0), jnp.where(low_half, mix_lo, 0.0),
        jnp.where(low_half, 0.0, mix_hi), jnp.where(low_half, 0.0, mix_lo)], axis=0).astype(BF16)

    loads["wg"].wait()
    loads["wu"].wait()
    loads["wd"].wait()
    def experts(lo, hi):
        count = hi - lo
        tokens = arrived[lo:hi].astype(F32).reshape(count, 2, RES, 1024)
        tokens = join(tokens[:, 0].reshape(count * RES, 1024), tokens[:, 1].reshape(count * RES, 1024)).astype(BF16)
        which = (iota((count * RES, FFL), 0) % RES) // 4
        inner = []
        for e in range(2):
            gate = dot(tokens, wg[e])
            up = dot(tokens, wu[e])
            act = gate / (1.0 + jnp.exp(-gate)) * up
            inner.append(jnp.where(which == e, act, 0.0).astype(BF16))
        out = dot(inner[0], wd[0]) + dot(inner[1], wd[1])
        out = [part.reshape(count, RES, 1024) for part in split(out)]
        ret_send[lo:hi] = jnp.concatenate(out, axis=1).astype(BF16)

    def give_back(g):
        lo, hi = NEAR[g]
        return launch(lo, hi, lambda n: ret_send.at[n], lambda n: ret.at[n], r_ss.at[g], r_rs.at[g], behind)

    swaps = []
    for g, (lo, hi) in enumerate(FAR):
        far_moves[g][0]()
        swaps.append(head_exchange(
            lambda p: arrived.at[pl.ds(lo, hi - lo), :, quarter(head)],
            lambda p: arrived.at[pl.ds(lo, hi - lo), :, quarter(p)], y_ss.at[g], y_rs.at[g]))
    returns = []

    def near(g):
        lo, hi = NEAR[g]
        moves[g][0]()
        experts(lo, hi)
        returns.append(give_back(g))

    near(0)
    parts = []
    for g, (lo, hi) in enumerate(FAR):
        swaps[g][0]()
        experts(lo, hi)
        parts.append(head_exchange(
            lambda p: ret_send.at[pl.ds(lo, hi - lo), :, quarter(p)],
            lambda p: part_all.at[p, pl.ds(lo, hi - lo)], p_ss.at[g], p_rs.at[g]))
        part_all[head, lo:hi] = ret_send[lo:hi, :, quarter(head)]
    near(1)
    ret[NREQ - 1] = ret_send[NREQ - 1]
    far_returns = []
    for g, (lo, hi) in enumerate(FAR):
        parts[g][0]()
        whole = [part_all[h, lo:hi].astype(F32) for h in range(NHEAD)]
        far_send[lo:hi] = ((whole[0] + whole[1]) + (whole[2] + whole[3])).astype(BF16)
        far_returns.append(launch(
            lo, hi, lambda n: far_send.at[n], lambda n: far_ret.at[n], t_ss.at[g], t_rs.at[g], behind))
    for back_move in returns:
        back_move[0]()
    mixed = dot(mix[:, FIRST * ROWS:], ret[FIRST:].reshape(wide - FIRST * ROWS, 1024))
    mixture = join(mixed[0:16] + mixed[16:32], mixed[32:48] + mixed[48:64])
    for h in range(NHEAD):
        fin_send[h] = mixture[:, h * WIDTH:(h + 1) * WIDTH].astype(BF16)
    f_recv, f_sent = head_exchange(lambda p: fin_send.at[p], lambda p: fin_all.at[p], f_ss, f_rs)
    fin_all[head] = fin_send[head]
    for group in swaps + parts + far_moves + moves + returns:
        group[1]()
    own = resid[:, pl.ds(pl.multiple_of(head * WIDTH, WIDTH), WIDTH)]
    f_recv()
    total = own + ((fin_all[0].astype(F32) + fin_all[1].astype(F32))
                   + (fin_all[2].astype(F32) + fin_all[3].astype(F32)))
    for group in far_returns:
        group[0]()
    mixed = dot(mix[:, :FIRST * ROWS], far_ret[...].reshape(FIRST * ROWS, 256))
    total = total + jnp.concatenate([mixed[0:16] + mixed[16:32], mixed[32:48] + mixed[48:64]], axis=1)
    out_ref[...] = total.astype(BF16)
    f_sent()
    for group in far_returns:
        group[1]()


def body(hidden_in, gain_attn, gain_moe, w_query, w_key, w_value, w_out, w_router, w_gate, w_up, w_down,
         cache_kv, parked_kv, lengths, cache_source, expert_ids):
    half = HD // 2
    freq = 50000.0 ** (-2.0 * np.arange(half, dtype=np.float64) / HD)
    table = np.zeros((8, NREQ * ROWS), np.float32)
    table[0, :HD] = np.concatenate([freq, freq])
    table[1:4] = np.repeat(np.asarray(OFFSETS).T, ROWS, axis=1)
    table[4:7, :3 * NREQ] = np.tile(np.asarray(OFFSETS).T, (1, 3))
    hbm = pl.BlockSpec(memory_space=pl.ANY)
    dma = pltpu.SemaphoreType.DMA
    operands = [hidden_in, gain_attn.reshape(1, D), gain_moe.reshape(1, D), jnp.asarray(table),
                lengths.reshape(1, -1), cache_source.reshape(1, -1), expert_ids.T,
                w_query, w_key, w_value, w_out, w_router.T, w_gate, w_up, w_down, cache_kv, parked_kv]
    q_block = (NREQ, ROWS, 256)
    wide = (NREQ, ROWS, 1024)
    return pl.pallas_call(
        kernel,
        out_shape=jax.ShapeDtypeStruct((ROWS, WIDTH), BF16),
        in_specs=[hbm] * len(operands),
        out_specs=pl.BlockSpec(memory_space=pltpu.VMEM),
        scratch_shapes=[pltpu.VMEM(x.shape, x.dtype) for x in operands] + [
            pltpu.VMEM(q_block[1:], BF16), pltpu.VMEM(q_block, BF16),
            pltpu.VMEM(q_block[1:], BF16), pltpu.VMEM(q_block, BF16),
            pltpu.VMEM((1, HD), F32), pltpu.VMEM((NREQ, 1, HD), F32),
            pltpu.VMEM((NHEAD, ROWS, 1024), BF16), pltpu.VMEM((NHEAD, ROWS, 1024), BF16),
            pltpu.VMEM(wide, BF16), pltpu.VMEM(wide, BF16),
            pltpu.VMEM(wide, BF16), pltpu.VMEM(wide, BF16),
            pltpu.VMEM((NHEAD, FIRST, ROWS, 256), BF16),
            pltpu.VMEM((FIRST, ROWS, 256), BF16), pltpu.VMEM((FIRST, ROWS, 256), BF16),
            pltpu.VMEM((NHEAD, ROWS, WIDTH), BF16), pltpu.VMEM((NHEAD, ROWS, WIDTH), BF16),
            pltpu.VMEM((ROWS, D), F32),
            dma((len(operands),)),
            dma((1,)), dma((1,)), dma((2,)), dma((2,)),
            dma((2, NHEAD)), dma((2, NHEAD)),
            dma((4,)), dma((4,)), dma((2, NHEAD)), dma((2, NHEAD)), dma((2, NHEAD)), dma((2, NHEAD)),
            dma((2,)), dma((2,)), dma((2,)), dma((2,)),
            dma((NHEAD,)), dma((NHEAD,)),
        ],
        compiler_params=pltpu.CompilerParams(
            collective_id=0, has_side_effects=True, vmem_limit_bytes=60 * 1024 * 1024),
    )(*operands)


def solution(mesh):
    placed = (
        P("req", None),
        P(),
        P(),
        P(None, "head"),
        P(None, "head"),
        P(None, "head"),
        P("head", None),
        P(),
        P("req", None, "head"),
        P("req", None, "head"),
        P("req", "head", None),
        P(None, "req", None, "head"),
        P(None, "req", None, "head"),
        P(),
        P(),
        P("req", None),
    )
    return jax.shard_map(
        body, mesh=mesh, in_specs=placed, out_specs=P("req", "head"), check_vma=False
    )
```
